32 devices in a mesh: wide: 16 (over z, y, core), narrow: 2 (over x).
Axes of the slice: x: 2, y: 2, z: 4, core: 2. Of those that a mesh axis runs over, the one named last changes fastest.
Arguments:
- coeffs: bfloat16 [16384, 9216], P('wide', 'narrow'), may hold values from -6 to 6
- earlier: bfloat16 [16384, 2048], P('wide', 'narrow'), may hold values from -6 to 6
- inv_tiles: float32 [4, 128, 128], replicated, may hold values from -0.041666667 to 0.041666667
- piv_local: int32 [512], replicated, may hold values from 0 to 1023
- piv_owner: int32 [512, 1], replicated, may hold values from 0 to 15; in each aligned block of 512 rows (0 to 511, 512 to 1023, ...) at most 96 rows name the same one
Outputs:
- new_columns: float32 [16384, 512], P('wide', 'narrow')
The draws below stay inside these ranges and needn't reach their ends.
Inputs may be any that keep to these rules, and one draw needn't show every extreme that they name: `piv_owner`: each index of wide owns at most 96 of the 512 pivots, and some index owns exactly 96.
All inputs are finite; a program needn't handle non-finite values.
Results may differ from the reference program's by a relative error of at most 0.0003.
Values may be sent and summed in bfloat16 or wider, within the bound.
No kernel may reach another device: no remote copies, remote signals or barrier semaphores. Data moves between devices by JAX's collectives and lax.ppermute only.
A program may use at most 64 MiB of HBM per device.

```python
import math
import jax
import jax.numpy as jnp
import numpy as np
from jax import lax

NOCC = 9216
PANEL = 512
BLOCK = 128
ROWS_DEV = 1024
KPREV = 2048
NBLK = 4
NAO = 16384
CAP = 96
N_WIDE = 16


def draw_inv_tiles(key, part):
    key_diag = jax.random.fold_in(key, 11)
    key_off = jax.random.fold_in(key, 12)
    tile_scale = 1.0 / jnp.sqrt(jnp.float32(NOCC))
    identity = jnp.eye(BLOCK, dtype=jnp.float32)
    diag_vals = jnp.exp(jax.random.uniform(key_diag, (NBLK, BLOCK), jnp.float32, math.log(0.5), math.log(2.0)))
    spread = jax.random.truncated_normal(key_off, -4.0, 4.0, (NBLK, BLOCK, BLOCK), jnp.float32)
    offdiag = spread * (0.4 / math.sqrt(BLOCK)) * (1.0 - identity)
    return ((identity * diag_vals[:, :, None] + offdiag) * tile_scale).astype(jnp.float32)


def set_ends(values, stream_key, low, top_value):
    dims = values.shape
    spot = [jax.random.randint(jax.random.fold_in(stream_key, axis), (), 0, dims[axis]) for axis in range(len(dims))]
    values = values.at[tuple(spot)].set(low)
    longest = dims.index(max(dims))
    spot[longest] = (spot[longest] + 1) % dims[longest]
    return values.at[tuple(spot)].set(top_value)


def level_of(rng, shape, cuts, least, high):
    def one(dim, shards_of):
        heights = jax.random.uniform(jax.random.fold_in(jax.random.fold_in(rng, 6), dim), (shards_of,), jnp.float32, least / len(cuts), high / len(cuts))
        return jnp.repeat(jnp.exp(heights), shape[dim] // shards_of).reshape((-1,) + (1,) * (len(shape) - dim - 1))

    gain = one(*cuts[0])
    for cut in cuts[1:]:
        gain = gain * one(*cut)
    return gain


def assign_block(key, own, number, rows, number_of, top, bound, slope):
    order = jax.random.permutation(key, number_of)
    crowded, usual = portions_of(number_of, rows * top, bound, slope, True), portions_of(number_of, rows * top, bound, slope, False)
    places = jnp.arange(number_of)

    def named(sizes, rotation):
        used = int((sizes > 0).sum())
        fixed = max(1, used // 4)
        shifted = fixed + (places - fixed + rotation * (used - fixed)) % max(1, number_of - fixed)
        return jnp.zeros((number_of,), jnp.int32).at[order[jnp.where(places < fixed, places, shifted)]].set(jnp.asarray(sizes, jnp.int32))

    sizes = jnp.where(number % 4 == 0, named(crowded, number // 4), named(usual, number - number // 4 - 1))
    mixed = jax.random.permutation(jax.random.fold_in(own, 3), number_of)
    source_of, taker = mixed[0:number_of // 2 * 2:2], mixed[1:number_of // 2 * 2:2]
    room = jnp.minimum(sizes[source_of] - 1, bound - sizes[taker]) // 2
    room = jnp.where((source_of == order[0]) | (taker == order[0]) | (sizes[taker] == 0), 0, jnp.maximum(room, 0))
    shifted = jax.random.randint(jax.random.fold_in(own, 4), (number_of // 2,), 0, 1 << 20) % (room + 1)
    sizes = sizes.at[source_of].add(-shifted).at[taker].add(shifted)
    labels = jnp.searchsorted(jnp.cumsum(sizes), jnp.arange(rows * top), side="right").astype(jnp.int32)
    table = labels.reshape(top, rows).T
    table = table[jax.random.permutation(jax.random.fold_in(own, 1), rows)]
    rotation = jax.random.randint(jax.random.fold_in(own, 2), (rows, 1), 0, top)
    return jnp.take_along_axis(table, (jnp.arange(top)[None, :] + rotation) % top, axis=1)


def portions_of(amount, total, limit, skew, full):
    loads = [(1 << 20) // math.isqrt(rank ** skew) + 1 for rank in range(1, amount + 1)]
    largest = limit if full else min(limit, max(-(-total // amount), total * loads[0] // sum(loads)))
    least = 1 if total - largest >= amount - 1 else 0
    counts, rest = [largest] + [least] * (amount - 1), total - largest - least * (amount - 1)
    while rest > 0:
        free = [i for i in range(1, amount) if counts[i] < largest] or [i for i in range(1, amount) if counts[i] < limit]
        whole, remaining = sum([loads[i] for i in free]), rest
        for i in free:
            extra = min(limit - counts[i], max(1, remaining * loads[i] // whole), rest)
            counts[i] = counts[i] + extra
            rest = rest - extra
    return np.array(counts)


def normal_values(own_key, shape, scale, reach, split=(), kind=jnp.bfloat16):
    array = scale * jax.random.normal(own_key, shape, jnp.float32)
    if split:
        array = array * level_of(own_key, shape, split, -0.22, 0.18)
    return jnp.clip(array, -reach, reach).astype(kind)


def setup_inputs(seed: int = 0) -> dict:
    keys = jax.random.split(jax.random.key(seed), 6)
    coeffs = normal_values(keys[0], (NAO, NOCC), 1.0, 6.0, ((0, 16), (1, 2)))
    earlier = normal_values(keys[1], (NAO, KPREV), 1.0, 6.0, ((0, 16), (1, 2)))
    inv_tiles = draw_inv_tiles(jax.random.fold_in(keys[5], 71), 0)
    piv_local = set_ends(jax.random.randint(keys[3], (PANEL,), 0, ROWS_DEV), jax.random.fold_in(keys[3], 1), 0, ROWS_DEV - 1).astype(jnp.int32)
    piv_owner_keys = jax.random.split(jax.random.fold_in(keys[4], 1), PANEL // PANEL)
    piv_owner_turns = jax.random.permutation(jax.random.fold_in(keys[4], 3), PANEL // PANEL)
    piv_owner = jax.vmap(lambda own, number: assign_block(jax.random.fold_in(keys[4], 2), own, number, PANEL, N_WIDE, 1, CAP, 2))(piv_owner_keys, piv_owner_turns).reshape((PANEL, 1))
    return {"coeffs": coeffs, "earlier": earlier, "inv_tiles": inv_tiles, "piv_local": piv_local, "piv_owner": piv_owner}


def panel_factor(density, diag_block, inv_tiles):
    block_size = inv_tiles.shape[1]
    piv_parts = []
    new_parts = []
    for block_index in range(inv_tiles.shape[0]):
        low_edge = block_index * block_size
        high_edge = low_edge + block_size
        piv_rest = diag_block[:, low_edge:high_edge]
        new_rest = density[:, low_edge:high_edge]
        if block_index > 0:
            piv_left = jnp.concatenate(piv_parts, axis=1)
            new_left = jnp.concatenate(new_parts, axis=1)
            coupling = piv_left[low_edge:high_edge]
            piv_rest = piv_rest - jnp.dot(piv_left, coupling.T, precision=lax.Precision.HIGHEST)
            new_rest = new_rest - jnp.dot(new_left, coupling.T, precision=lax.Precision.HIGHEST)
        piv_parts.append(jnp.dot(piv_rest, inv_tiles[block_index], precision=lax.Precision.HIGHEST))
        new_parts.append(jnp.dot(new_rest, inv_tiles[block_index], precision=lax.Precision.HIGHEST))
    return jnp.concatenate(new_parts, axis=1)


def reference(coeffs, earlier, inv_tiles, piv_local, piv_owner):
    global_rows = (piv_owner[:, 0] * ROWS_DEV + piv_local).astype(jnp.int32)
    pivot_coeffs = coeffs[global_rows]
    pivot_earlier = earlier[global_rows]
    density = jnp.dot(coeffs, pivot_coeffs.T, preferred_element_type=jnp.float32)
    density = density - jnp.dot(earlier, pivot_earlier.T, preferred_element_type=jnp.float32)
    diag_block = density[global_rows]
    return panel_factor(density, diag_block, inv_tiles)
```

```python
import jax
import jax.numpy as jnp
from jax import lax
from jax.sharding import PartitionSpec as P

LANES = 128
GROUP = 4
EXACT = lax.Precision.HIGHEST


def panel_factor(density, diag_block, inv_tiles):
    block_size = inv_tiles.shape[1]
    piv_parts = []
    new_parts = []
    for block_index in range(inv_tiles.shape[0]):
        low_edge = block_index * block_size
        high_edge = low_edge + block_size
        piv_rest = diag_block[:, low_edge:high_edge]
        new_rest = density[:, low_edge:high_edge]
        if block_index > 0:
            piv_left = jnp.concatenate(piv_parts, axis=1)
            new_left = jnp.concatenate(new_parts, axis=1)
            coupling = piv_left[low_edge:high_edge]
            piv_rest = piv_rest - jnp.dot(piv_left, coupling.T, precision=EXACT)
            new_rest = new_rest - jnp.dot(new_left, coupling.T, precision=EXACT)
        piv_parts.append(jnp.dot(piv_rest, inv_tiles[block_index], precision=EXACT))
        new_parts.append(jnp.dot(new_rest, inv_tiles[block_index], precision=EXACT))
    return jnp.concatenate(new_parts, axis=1)


def general(coeffs, earlier, inv_tiles, piv_local, piv_owner):
    owners = piv_owner[:, 0]
    panel_width = piv_local.shape[0]
    mine = owners == lax.axis_index("wide")
    capacity = 3 * panel_width // lax.axis_size("wide")
    positions = jnp.arange(panel_width, dtype=jnp.int32)
    same_owner = owners[:, None] == owners[None, :]
    before = positions[None, :] < positions[:, None]
    slot_rank = jnp.sum(same_owner & before, axis=1)
    slot_index = owners * capacity + slot_rank
    wanted = mine[None, :] & (slot_rank[None, :] == jnp.arange(capacity, dtype=jnp.int32)[:, None])
    local_rows = jnp.sum(jnp.where(wanted, piv_local[None, :], 0), axis=1)
    filled = jnp.any(wanted, axis=1)
    slots = [jnp.where(filled[:, None], source[local_rows], 0) for source in (coeffs, earlier)]
    pieces = [lax.all_gather(slot, "wide", axis=0, tiled=True) for slot in slots]
    select = slot_index[:, None] == jnp.arange(pieces[0].shape[0], dtype=jnp.int32)[None, :]
    select = select.astype(jnp.bfloat16)
    pivots = [
        jnp.dot(select, piece, preferred_element_type=jnp.float32).astype(jnp.bfloat16)
        for piece in pieces
    ]
    partial = [
        jnp.einsum("ro,po->rp", source, pivot, preferred_element_type=jnp.float32)
        for source, pivot in zip((coeffs, earlier), pivots)
    ]
    density = lax.psum_scatter(
        partial[0] - partial[1], "narrow", scatter_dimension=0, tiled=True
    )
    diag = [
        jnp.einsum("qo,po->qp", pivot, pivot, preferred_element_type=jnp.float32)
        for pivot in pivots
    ]
    diag_block = lax.psum(diag[0] - diag[1], "narrow")
    factor = panel_factor(density, diag_block, inv_tiles)
    return lax.all_to_all(factor, "narrow", split_axis=1, concat_axis=0, tiled=True)


def arrival_order(lines):
    tables = []
    for line in range(lines):
        order = []
        for hop in range(1, lines):
            sides = ("up", "down") if 2 * line < lines else ("down", "up")
            for side in sides:
                source = line + hop if side == "up" else line - hop
                if 0 <= source < lines:
                    order.append((side, hop, source))
        tables.append(order)
    return tables


def pick(index, table, choices):
    names = [table[line] for line in range(len(table))]
    result = choices[names[-1]]
    for line in range(len(table) - 1):
        if names[line] != names[-1]:
            result = jnp.where(index == line, choices[names[line]], result)
    return result


def exchange(value, axis, bit, size):
    return lax.ppermute(value, axis, [(i, i ^ bit) for i in range(size)])


def own_rows(coeffs, earlier, piv_local, owners, ranks, capacity):
    me = lax.axis_index("wide")
    slots = jnp.arange(capacity, dtype=jnp.int32)
    wanted = (owners == me)[None, :] & (ranks[None, :] == slots[:, None])
    local_rows = jnp.sum(jnp.where(wanted, piv_local[None, :] + 1, 0), axis=1) - 1
    rows = jnp.arange(coeffs.shape[0], dtype=jnp.int32)
    select = (local_rows[:, None] == rows[None, :]).astype(jnp.bfloat16)
    return [
        jnp.dot(select, source, preferred_element_type=jnp.float32).astype(jnp.bfloat16)
        for source in (coeffs, earlier)
    ]


def lined(coeffs, earlier, inv_tiles, piv_local, piv_owner):
    size = lax.axis_size("wide")
    lines = size // GROUP
    me = lax.axis_index("wide")
    line = me // GROUP
    lane = me % GROUP
    panel = piv_local.shape[0]
    block = inv_tiles.shape[1]
    blocks = inv_tiles.shape[0]
    capacity = 3 * panel // size
    width = coeffs.shape[1] // ((lines - 1) * GROUP)
    short = earlier.shape[1] // GROUP
    span = GROUP * width

    owners = piv_owner[:, 0]
    positions = jnp.arange(panel, dtype=jnp.int32)
    earlier_same = (owners[:, None] == owners[None, :]) & (positions[None, :] < positions[:, None])
    ranks = jnp.sum(earlier_same, axis=1, dtype=jnp.int32)
    slots_coeffs, slots_earlier = own_rows(coeffs, earlier, piv_local, owners, ranks, capacity)
    parts = [slots_coeffs[:, i * width : (i + 1) * width] for i in range((lines - 1) * GROUP)]
    parts += [
        jnp.pad(slots_earlier[:, i * short : (i + 1) * short], ((0, 0), (0, width - short)))
        for i in range(GROUP)
    ]
    parts = jnp.stack(parts)

    got = []
    for bit in range(size):
        piece = lax.dynamic_index_in_dim(parts, me ^ bit, 0, keepdims=False)
        got.append(exchange(piece, "wide", bit, size) if bit else piece)
    stacked = jnp.concatenate(got, axis=0)
    places = (owners ^ me) * capacity + ranks
    choose = places[:, None] == jnp.arange(size * capacity, dtype=jnp.int32)[None, :]
    own = jnp.dot(choose.astype(jnp.bfloat16), stacked, preferred_element_type=jnp.float32)
    own = own.astype(jnp.bfloat16)

    both = jnp.concatenate(
        [coeffs, jnp.pad(earlier, ((0, 0), (0, span - earlier.shape[1])))], axis=1
    )
    up, down = own, own
    tables = arrival_order(lines)
    received = {}
    pieces = [own]
    for hop in range(1, lines):
        rising = [(i, i + GROUP) for i in range(size - GROUP) if i // GROUP >= hop - 1]
        falling = [(i, i - GROUP) for i in range(GROUP, size) if lines - 1 - i // GROUP >= hop - 1]
        down = lax.ppermute(down, "wide", rising)
        up = lax.ppermute(up, "wide", falling)
        received[("down", hop)] = down
        received[("up", hop)] = up
        pieces.append(pick(line, [tables[i][hop - 1][:2] for i in range(lines)], received))
    sources = [line]
    for hop in range(1, lines):
        sources.append(pick(line, list(range(lines)), [jnp.int32(tables[i][hop - 1][2]) for i in range(lines)]))

    partial = 0.0
    diag = 0.0
    for piece, source in zip(pieces, sources):
        across = exchange(piece, "wide", 2, size)
        beside = exchange(piece, "wide", 1, size)
        corner = exchange(across, "wide", 1, size)
        odd = (lane & 1) == 1
        high = (lane & 2) == 2
        near = jnp.concatenate([jnp.where(odd, beside, piece), jnp.where(odd, piece, beside)], axis=1)
        far = jnp.concatenate([jnp.where(odd, corner, across), jnp.where(odd, across, corner)], axis=1)
        pivots = jnp.concatenate([jnp.where(high, far, near), jnp.where(high, near, far)], axis=1)
        if width != short:
            packed = jnp.concatenate(
                [pivots[:, i * width : i * width + short] for i in range(GROUP)], axis=1
            )
            packed = jnp.pad(packed, ((0, 0), (0, span - GROUP * short)))
            pivots = jnp.where(source == lines - 1, packed, pivots)
        signed = jnp.where(source == lines - 1, -pivots, pivots)
        columns = lax.dynamic_slice_in_dim(both, source * span, span, axis=1)
        partial = partial + jnp.einsum("ro,po->rp", columns, signed, preferred_element_type=jnp.float32)
        diag = diag + jnp.einsum("qo,po->qp", pivots, signed, preferred_element_type=jnp.float32)

    lower = [
        diag[i * block : (i + 1) * block, j * block : (j + 1) * block]
        for i in range(blocks)
        for j in range(i)
    ]
    lower = jnp.stack(lower)
    odd = (lane & 1) == 1
    half = lower.shape[0] // 2
    mine = jnp.where(odd, lower[half:], lower[:half])
    mine = mine + exchange(mine, "narrow", 1, 2)
    other = exchange(mine, "wide", 1, size)
    lower = jnp.concatenate([jnp.where(odd, other, mine), jnp.where(odd, mine, other)], axis=0)

    def diag_at(i, j):
        return lower[i * (i - 1) // 2 + j]

    factor = {}
    new = []
    for j in range(blocks):
        rest = partial[:, j * block : (j + 1) * block]
        for k in range(j):
            rest = rest - jnp.dot(new[k], factor[(j, k)].T, precision=EXACT)
        new.append(jnp.dot(rest, inv_tiles[j], precision=EXACT))
        for i in range(j + 1, blocks):
            rest = diag_at(i, j)
            for k in range(j):
                rest = rest - jnp.dot(factor[(i, k)], factor[(j, k)].T, precision=EXACT)
            factor[(i, j)] = jnp.dot(rest, inv_tiles[j], precision=EXACT)
    first = jnp.concatenate(new[: blocks // 2], axis=1)
    second = jnp.concatenate(new[blocks // 2 :], axis=1)
    right = lax.axis_index("narrow") == 1
    keep = jnp.where(right, second, first)
    give = jnp.where(right, first, second)
    return keep + exchange(give, "narrow", 1, 2)


def on_device(coeffs, earlier, inv_tiles, piv_local, piv_owner):
    size = lax.axis_size("wide")
    lines = size // GROUP
    parts = (lines - 1) * GROUP
    fits = (
        size == lines * GROUP
        and size & (size - 1) == 0
        and lines > 1
        and lax.axis_size("narrow") == 2
        and coeffs.shape[1] % (parts * LANES) == 0
        and earlier.shape[1] % (GROUP * LANES) == 0
        and earlier.shape[1] * parts <= coeffs.shape[1] * GROUP
        and inv_tiles.shape[0] % 4 == 0
    )
    chosen = lined if fits else general
    return chosen(coeffs, earlier, inv_tiles, piv_local, piv_owner)


def solution(mesh):
    return jax.shard_map(
        on_device,
        mesh=mesh,
        in_specs=(P("wide", "narrow"), P("wide", "narrow"), P(), P(), P()),
        out_specs=P("wide", "narrow"),
        check_vma=False,
    )
```

```python
import functools

import jax
import jax.numpy as jnp
from jax import lax
from jax.experimental import pallas as pl
from jax.experimental.pallas import tpu as pltpu
from jax.sharding import PartitionSpec as P


LANES = 128
GROUP = 4
TILES = 2
EXACT = lax.Precision.HIGHEST


def panel_factor(density, diag_block, inv_tiles):
    block_size = inv_tiles.shape[1]
    piv_parts = []
    new_parts = []
    for block_index in range(inv_tiles.shape[0]):
        low_edge = block_index * block_size
        high_edge = low_edge + block_size
        piv_rest = diag_block[:, low_edge:high_edge]
        new_rest = density[:, low_edge:high_edge]
        if block_index > 0:
            piv_left = jnp.concatenate(piv_parts, axis=1)
            new_left = jnp.concatenate(new_parts, axis=1)
            coupling = piv_left[low_edge:high_edge]
            piv_rest = piv_rest - jnp.dot(piv_left, coupling.T, precision=EXACT)
            new_rest = new_rest - jnp.dot(new_left, coupling.T, precision=EXACT)
        piv_parts.append(jnp.dot(piv_rest, inv_tiles[block_index], precision=EXACT))
        new_parts.append(jnp.dot(new_rest, inv_tiles[block_index], precision=EXACT))
    return jnp.concatenate(new_parts, axis=1)


def general(coeffs, earlier, inv_tiles, piv_local, piv_owner):
    owners = piv_owner[:, 0]
    panel_width = piv_local.shape[0]
    mine = owners == lax.axis_index("wide")
    capacity = 3 * panel_width // lax.axis_size("wide")
    positions = jnp.arange(panel_width, dtype=jnp.int32)
    same_owner = owners[:, None] == owners[None, :]
    before = positions[None, :] < positions[:, None]
    slot_rank = jnp.sum(same_owner & before, axis=1)
    slot_index = owners * capacity + slot_rank
    wanted = mine[None, :] & (slot_rank[None, :] == jnp.arange(capacity, dtype=jnp.int32)[:, None])
    local_rows = jnp.sum(jnp.where(wanted, piv_local[None, :], 0), axis=1)
    filled = jnp.any(wanted, axis=1)
    slots = [jnp.where(filled[:, None], source[local_rows], 0) for source in (coeffs, earlier)]
    pieces = [lax.all_gather(slot, "wide", axis=0, tiled=True) for slot in slots]
    select = slot_index[:, None] == jnp.arange(pieces[0].shape[0], dtype=jnp.int32)[None, :]
    select = select.astype(jnp.bfloat16)
    pivots = [
        jnp.dot(select, piece, preferred_element_type=jnp.float32).astype(jnp.bfloat16)
        for piece in pieces
    ]
    partial = [
        jnp.einsum("ro,po->rp", source, pivot, preferred_element_type=jnp.float32)
        for source, pivot in zip((coeffs, earlier), pivots)
    ]
    density = lax.psum_scatter(
        partial[0] - partial[1], "narrow", scatter_dimension=0, tiled=True
    )
    diag = [
        jnp.einsum("qo,po->qp", pivot, pivot, preferred_element_type=jnp.float32)
        for pivot in pivots
    ]
    diag_block = lax.psum(diag[0] - diag[1], "narrow")
    factor = panel_factor(density, diag_block, inv_tiles)
    return lax.all_to_all(factor, "narrow", split_axis=1, concat_axis=0, tiled=True)


def arrival_order(lines):
    tables = []
    for line in range(lines):
        order = []
        for hop in range(1, lines):
            sides = ("up", "down") if 2 * line < lines else ("down", "up")
            for side in sides:
                source = line + hop if side == "up" else line - hop
                if 0 <= source < lines:
                    order.append((side, hop, source))
        tables.append(order)
    return tables


def look_up(table, line):
    result = jnp.int32(table[-1])
    for index, entry in enumerate(table[:-1]):
        result = jnp.where(line == index, jnp.int32(entry), result)
    return result


def exchange(value, axis, bit, size):
    return lax.ppermute(value, axis, [(i, i ^ bit) for i in range(size)])


def own_rows(coeffs, earlier, piv_local, owners, ranks, capacity):
    me = lax.axis_index("wide")
    slots = jnp.arange(capacity, dtype=jnp.int32)
    wanted = (owners == me)[None, :] & (ranks[None, :] == slots[:, None])
    local_rows = jnp.sum(jnp.where(wanted, piv_local[None, :] + 1, 0), axis=1) - 1
    rows = jnp.arange(coeffs.shape[0], dtype=jnp.int32)
    select = (local_rows[:, None] == rows[None, :]).astype(jnp.bfloat16)
    return [
        jnp.dot(chosen, source, preferred_element_type=jnp.float32).astype(jnp.bfloat16)
        for chosen, source in ((select, coeffs), (-select, earlier))
    ]


def accumulate_kernel(tables, shape, seat_ref, coeffs_ref, earlier_ref, *refs):
    width, short, tile, fresh = shape
    count = len(tables)
    groups = [refs[g * GROUP : (g + 1) * GROUP] for g in range(count)]
    refs = refs[count * GROUP :]
    if fresh:
        sum_ref, held_ref, main_ref, sems, hold_sems = refs
    else:
        old_sum_ref, sum_ref, held_ref, main_ref, sems, hold_sems = refs
    line, lane = seat_ref[0], seat_ref[1]
    tiles = main_ref.shape[0] // tile
    depth = width * GROUP
    lines = [look_up(table, line) for table in tables]
    final = len(tables[0]) - 1

    def rows_load(g, step):
        rows_at = pl.ds(step * tile, tile)
        base = pl.multiple_of(lines[g] * depth, LANES)
        return pltpu.make_async_copy(
            coeffs_ref.at[rows_at, pl.ds(base, depth)],
            main_ref.at[rows_at, pl.ds(g * depth, depth)], sems.at[g, step]
        )

    def short_loads(g, step):
        rows_at = pl.ds(step * tile, tile)
        return [
            pltpu.make_async_copy(
                earlier_ref.at[rows_at, pl.ds(index * short, short)],
                main_ref.at[rows_at, pl.ds(g * depth + index * width, short)],
                sems.at[g, step],
            )
            for index in range(GROUP)
        ]

    holds = []
    for g, pieces in enumerate(groups):
        for index, piece in enumerate(pieces):
            start = pl.multiple_of(g * depth + (lane ^ index) * width, LANES)
            holds.append(
                pltpu.make_async_copy(
                    piece, held_ref.at[pl.ds(start, width), :], hold_sems.at[g, index]
                )
            )
    for copy in holds:
        copy.start()
    for step in range(tiles):
        for g in range(count):

            @pl.when(lines[g] != final)
            def _():
                rows_load(g, step).start()

            @pl.when(lines[g] == final)
            def _():
                for copy in short_loads(g, step):
                    copy.start()

    if width != short:
        for g in range(count):

            @pl.when(lines[g] == final)
            def _():
                for index in range(GROUP):
                    start = g * depth + index * width
                    gap = slice(start + short, start + width)
                    main_ref[:, gap] = jnp.zeros((tiles * tile, width - short), jnp.bfloat16)

    for copy in holds:
        copy.wait()
    for step in range(tiles):
        rows_at = slice(step * tile, (step + 1) * tile)
        for g in range(count):

            @pl.when(lines[g] != final)
            def _():
                rows_load(g, step).wait()

            @pl.when(lines[g] == final)
            def _():
                for copy in short_loads(g, step):
                    copy.wait()

        total = jnp.dot(main_ref[rows_at, :], held_ref[...], preferred_element_type=jnp.float32)
        sum_ref[rows_at, :] = total if fresh else old_sum_ref[rows_at, :] + total


def accumulate(tables, seat, coeffs, earlier, groups, state):
    rows = coeffs.shape[0]
    width, panel = groups[0][0].shape
    short = earlier.shape[1] // GROUP
    tile = rows // TILES
    fresh = state is None
    count = len(groups)
    anywhere = pl.BlockSpec(memory_space=pl.ANY)
    vmem = pl.BlockSpec(memory_space=pltpu.VMEM)
    kernel = functools.partial(accumulate_kernel, tables, (width, short, tile, fresh))
    pieces = [piece for group in groups for piece in group]
    return pl.pallas_call(
        kernel,
        in_specs=[pl.BlockSpec(memory_space=pltpu.SMEM)]
        + [anywhere] * (2 + len(pieces))
        + ([] if fresh else [vmem]),
        out_specs=vmem,
        scratch_shapes=[
            pltpu.VMEM((count * width * GROUP, panel), jnp.bfloat16),
            pltpu.VMEM((rows, count * width * GROUP), jnp.bfloat16),
            pltpu.SemaphoreType.DMA((count, TILES)),
            pltpu.SemaphoreType.DMA((count, GROUP)),
        ],
        out_shape=jax.ShapeDtypeStruct((rows, panel), jnp.float32),
        input_output_aliases={} if fresh else {3 + len(pieces): 0},
        cost_estimate=pl.CostEstimate(
            flops=2 * rows * panel * width * len(pieces),
            bytes_accessed=2 * rows * width * len(pieces),
            transcendentals=0,
        ),
        name="accumulate",
    )(seat, coeffs, earlier, *pieces, *([] if fresh else [state]))


def choose(line, table, received):
    names = sorted(set(table))
    values = lax.optimization_barrier(tuple(received[name] for name in names))
    result = values[-1]
    for index, name in enumerate(names[:-1]):
        here = False
        for place, entry in enumerate(table):
            if entry == name:
                here = here | (line == place)
        result = jnp.where(here, values[index], result)
    return result


def split(value):
    high = value.astype(jnp.bfloat16)
    return high, (value - high.astype(jnp.float32)).astype(jnp.bfloat16)


def dot_split(left, right):
    left = jnp.concatenate([left[0], left[0], left[1]], axis=1)
    right = jnp.concatenate([right[0], right[1], right[0]], axis=0)
    return jnp.dot(left, right, preferred_element_type=jnp.float32)


def recur_kernel(blocks, side_ref, partial_ref, lower_ref, inv_ref, keep_ref, give_ref):
    block = inv_ref.shape[1]
    inverse = [split(inv_ref[j]) for j in range(blocks)]

    def stack(parts, axis):
        return tuple(jnp.concatenate(side, axis=axis) for side in zip(*parts))

    def flip(part):
        return tuple(jnp.transpose(side) for side in part)

    factor = {}
    for j in range(blocks - 1):
        rest = jnp.concatenate(
            [lower_ref[i * (i - 1) // 2 + j] for i in range(j + 1, blocks)], axis=0
        )
        if j:
            left = stack([stack([factor[i, k] for k in range(j)], 1) for i in range(j + 1, blocks)], 0)
            right = stack([flip(factor[j, k]) for k in range(j)], 0)
            rest = rest - dot_split(left, right)
        made = split(dot_split(split(rest), inverse[j]))
        for i in range(j + 1, blocks):
            rows = slice((i - j - 1) * block, (i - j) * block)
            factor[i, j] = (made[0][rows], made[1][rows])
    new = []
    for j in range(blocks):
        rest = partial_ref[:, j * block : (j + 1) * block]
        if j:
            right = stack([flip(factor[j, k]) for k in range(j)], 0)
            rest = rest - dot_split(stack(new, 1), right)
        result = dot_split(split(rest), inverse[j])
        new.append(split(result))
        half = blocks // 2
        mine = side_ref[0] == j // half
        place = pl.ds((j % half) * block, block)

        @pl.when(mine)
        def _():
            keep_ref[:, place] = result

        @pl.when(jnp.logical_not(mine))
        def _():
            give_ref[:, place] = result


def recur(partial, lower, inv_tiles):
    rows, panel = partial.shape
    blocks = inv_tiles.shape[0]
    half = jax.ShapeDtypeStruct((rows, panel // 2), jnp.float32)
    vmem = pl.BlockSpec(memory_space=pltpu.VMEM)
    return pl.pallas_call(
        functools.partial(recur_kernel, blocks),
        in_specs=[pl.BlockSpec(memory_space=pltpu.SMEM), vmem, vmem, vmem],
        out_specs=[vmem, vmem],
        out_shape=[half, half],
        name="recur",
    )(lax.axis_index("narrow")[None], partial, lower, inv_tiles)


def lined(*args):
    return lined_panel(*args)


def lined_panel(coeffs, earlier, inv_tiles, piv_local, piv_owner):
    size = lax.axis_size("wide")
    lines = size // GROUP
    me = lax.axis_index("wide")
    line = me // GROUP
    lane = me % GROUP
    panel = piv_local.shape[0]
    block = inv_tiles.shape[1]
    blocks = inv_tiles.shape[0]
    capacity = 3 * panel // size
    width = coeffs.shape[1] // ((lines - 1) * GROUP)
    short = earlier.shape[1] // GROUP

    owners = piv_owner[:, 0]
    positions = jnp.arange(panel, dtype=jnp.int32)
    earlier_same = (owners[:, None] == owners[None, :]) & (positions[None, :] < positions[:, None])
    ranks = jnp.sum(earlier_same, axis=1, dtype=jnp.int32)
    slots_coeffs, slots_earlier = own_rows(coeffs, earlier, piv_local, owners, ranks, capacity)
    parts = [slots_coeffs[:, i * width : (i + 1) * width] for i in range((lines - 1) * GROUP)]
    parts += [
        jnp.pad(slots_earlier[:, i * short : (i + 1) * short], ((0, 0), (0, width - short)))
        for i in range(GROUP)
    ]
    parts = jnp.stack(parts)

    got = []
    for bit in range(size):
        piece = lax.dynamic_index_in_dim(parts, me ^ bit, 0, keepdims=False)
        got.append(exchange(piece, "wide", bit, size) if bit else piece)
    stacked = jnp.concatenate(got, axis=0)
    places = (owners ^ me) * capacity + ranks
    taken = places[:, None] == jnp.arange(size * capacity, dtype=jnp.int32)[None, :]
    own = lax.dot_general(
        stacked,
        taken.astype(jnp.bfloat16),
        (((0,), (1,)), ((), ())),
        preferred_element_type=jnp.float32,
    ).astype(jnp.bfloat16)

    up, down = own, own
    tables = arrival_order(lines)
    received = {}
    pieces = [own]
    sources = [tuple(range(lines))]
    seat = jnp.stack([line, lane])
    for hop in range(1, lines):
        rising = [(i, i + GROUP) for i in range(size - GROUP) if i // GROUP >= hop - 1]
        falling = [(i, i - GROUP) for i in range(GROUP, size) if lines - 1 - i // GROUP >= hop - 1]
        down = lax.ppermute(down, "wide", rising)
        up = lax.ppermute(up, "wide", falling)
        received[("down", hop)] = down
        received[("up", hop)] = up
        pieces.append(choose(line, [tables[i][hop - 1][:2] for i in range(lines)], received))
        sources.append(tuple(tables[i][hop - 1][2] for i in range(lines)))

    groups = []
    diag = 0.0
    for piece, source in zip(pieces, sources):
        across = exchange(piece, "wide", 2, size)
        beside = exchange(piece, "wide", 1, size)
        corner = exchange(across, "wide", 1, size)
        groups.append([piece, beside, across, corner])
        sign = jnp.where(look_up(source, line) == lines - 1, -1.0, 1.0)
        term = 0.0
        for part in groups[-1]:
            term = term + lax.dot_general(
                part[:, block:],
                part[:, :-block],
                (((0,), (0,)), ((), ())),
                preferred_element_type=jnp.float32,
            )
        diag = diag + sign * term
    partial = accumulate(sources[:-1], seat, coeffs, earlier, groups[:-1], None)
    partial = accumulate(sources[-1:], seat, coeffs, earlier, groups[-1:], partial)

    lower = jnp.stack(
        [
            diag[(i - 1) * block : i * block, j * block : (j + 1) * block]
            for i in range(blocks)
            for j in range(i)
        ]
    )
    odd = (lane & 1) == 1
    half = lower.shape[0] // 2
    mine = jnp.where(odd, lower[half:], lower[:half])
    mine = mine + exchange(mine, "narrow", 1, 2)
    other = exchange(mine, "wide", 1, size)
    lower = jnp.concatenate([jnp.where(odd, other, mine), jnp.where(odd, mine, other)], axis=0)
    keep, give = recur(partial, lower, inv_tiles)
    return keep + exchange(give, "narrow", 1, 2)


def on_device(coeffs, earlier, inv_tiles, piv_local, piv_owner):
    chosen = lined if fits(coeffs, earlier, inv_tiles) else general
    return chosen(coeffs, earlier, inv_tiles, piv_local, piv_owner)


def fits(coeffs, earlier, inv_tiles):
    size = lax.axis_size("wide")
    lines = size // GROUP
    parts = (lines - 1) * GROUP
    return (
        size == lines * GROUP
        and size & (size - 1) == 0
        and lines > 1
        and lax.axis_size("narrow") == 2
        and coeffs.shape[0] % 16 == 0
        and coeffs.shape[1] % (parts * LANES) == 0
        and earlier.shape[1] % (GROUP * LANES) == 0
        and earlier.shape[1] * parts <= coeffs.shape[1] * GROUP
        and inv_tiles.shape[0] % 4 == 0
    )


def solution(mesh):
    return jax.shard_map(
        on_device,
        mesh=mesh,
        in_specs=(P("wide", "narrow"), P("wide", "narrow"), P(), P(), P()),
        out_specs=P("wide", "narrow"),
        check_vma=False,
    )
```

```python
import functools

import jax
import jax.numpy as jnp
from jax import lax
from jax.experimental import pallas as pl
from jax.experimental.pallas import tpu as pltpu
from jax.sharding import PartitionSpec as P


LANES = 128
SUBLANES = 16
GROUP = 4
ONE_CUT = True
SENDS = 2
TILES = 2
EXACT = lax.Precision.HIGHEST


def panel_factor(density, diag_block, inv_tiles):
    block_size = inv_tiles.shape[1]
    piv_parts = []
    new_parts = []
    for block_index in range(inv_tiles.shape[0]):
        low_edge = block_index * block_size
        high_edge = low_edge + block_size
        piv_rest = diag_block[:, low_edge:high_edge]
        new_rest = density[:, low_edge:high_edge]
        if block_index > 0:
            piv_left = jnp.concatenate(piv_parts, axis=1)
            new_left = jnp.concatenate(new_parts, axis=1)
            coupling = piv_left[low_edge:high_edge]
            piv_rest = piv_rest - jnp.dot(piv_left, coupling.T, precision=EXACT)
            new_rest = new_rest - jnp.dot(new_left, coupling.T, precision=EXACT)
        piv_parts.append(jnp.dot(piv_rest, inv_tiles[block_index], precision=EXACT))
        new_parts.append(jnp.dot(new_rest, inv_tiles[block_index], precision=EXACT))
    return jnp.concatenate(new_parts, axis=1)


def general(coeffs, earlier, inv_tiles, piv_local, piv_owner):
    owners = piv_owner[:, 0]
    panel_width = piv_local.shape[0]
    mine = owners == lax.axis_index("wide")
    capacity = 3 * panel_width // lax.axis_size("wide")
    positions = jnp.arange(panel_width, dtype=jnp.int32)
    same_owner = owners[:, None] == owners[None, :]
    before = positions[None, :] < positions[:, None]
    slot_rank = jnp.sum(same_owner & before, axis=1)
    slot_index = owners * capacity + slot_rank
    wanted = mine[None, :] & (slot_rank[None, :] == jnp.arange(capacity, dtype=jnp.int32)[:, None])
    local_rows = jnp.sum(jnp.where(wanted, piv_local[None, :], 0), axis=1)
    filled = jnp.any(wanted, axis=1)
    slots = [jnp.where(filled[:, None], source[local_rows], 0) for source in (coeffs, earlier)]
    pieces = [lax.all_gather(slot, "wide", axis=0, tiled=True) for slot in slots]
    select = slot_index[:, None] == jnp.arange(pieces[0].shape[0], dtype=jnp.int32)[None, :]
    select = select.astype(jnp.bfloat16)
    pivots = [
        jnp.dot(select, piece, preferred_element_type=jnp.float32).astype(jnp.bfloat16)
        for piece in pieces
    ]
    partial = [
        jnp.einsum("ro,po->rp", source, pivot, preferred_element_type=jnp.float32)
        for source, pivot in zip((coeffs, earlier), pivots)
    ]
    density = lax.psum_scatter(
        partial[0] - partial[1], "narrow", scatter_dimension=0, tiled=True
    )
    diag = [
        jnp.einsum("qo,po->qp", pivot, pivot, preferred_element_type=jnp.float32)
        for pivot in pivots
    ]
    diag_block = lax.psum(diag[0] - diag[1], "narrow")
    factor = panel_factor(density, diag_block, inv_tiles)
    return lax.all_to_all(factor, "narrow", split_axis=1, concat_axis=0, tiled=True)


def arrival_order(lines):
    tables = []
    for line in range(lines):
        order = []
        for hop in range(1, lines):
            sides = ("up", "down") if 2 * line < lines else ("down", "up")
            for side in sides:
                source = line + hop if side == "up" else line - hop
                if 0 <= source < lines:
                    order.append((side, hop, source))
        tables.append(order)
    return tables


def look_up(table, line):
    result = jnp.int32(table[-1])
    for index, entry in enumerate(table[:-1]):
        result = jnp.where(line == index, jnp.int32(entry), result)
    return result


def exchange(value, axis, bit, size):
    return lax.ppermute(value, axis, [(i, i ^ bit) for i in range(size)])


def lower_pairs(blocks):
    pairs = [(i, j) for i in range(blocks) for j in range(i)]
    half = len(pairs) // 2
    return pairs[:half], pairs[half:]


def near(values):
    return [pltpu.with_memory_space_constraint(value, pltpu.VMEM) for value in values]


def seat():
    me = lax.axis_index("wide")
    return lax.div(me, GROUP), lax.rem(me, GROUP)


def hold_copies(lane, pieces, held_ref, sems):
    width = pieces[0].shape[0]
    copies = []
    for index, piece in enumerate(pieces):
        start = pl.multiple_of((lane ^ index) * width, SUBLANES)
        target = held_ref.at[pl.ds(start, width), :]
        copies.append(pltpu.make_async_copy(piece, target, sems.at[index]))
    return copies


def add_lower(blocks, edge, lane, held_ref, old_ref, lower_ref):
    block = held_ref.shape[1] // blocks
    for parity, pairs in enumerate(lower_pairs(blocks)):

        @pl.when((lane & 1) == parity)
        def _():
            place = 0
            for i in sorted({pair[0] for pair in pairs}):
                picks = [pair[1] for pair in pairs if pair[0] == i]
                rows = slice(i * block, (i + 1) * block)
                columns = slice(picks[0] * block, (picks[-1] + 1) * block)
                terms = [
                    lax.dot_general(
                        held_ref[part, rows],
                        held_ref[part, columns],
                        (((0,), (0,)), ((), ())),
                        preferred_element_type=jnp.float32,
                    )
                    for part in (slice(0, edge), slice(edge, held_ref.shape[0]))
                ]
                total = terms[0] - terms[1]
                for index in range(len(picks)):
                    part = total[:, index * block : (index + 1) * block]
                    if old_ref is not None:
                        part = old_ref[place] + part
                    lower_ref[place] = part
                    place += 1


def lower_kernel(blocks, edge, bits, old_ref, *refs):
    pieces, lower_ref = refs[:-1], refs[-1]
    _, lane = seat()
    width, panel = pieces[0].shape
    block = panel // blocks
    signed = []
    for bit, piece in zip(bits, pieces):
        at = (lane ^ bit) * width + lax.broadcasted_iota(jnp.int32, (width, block), 0)
        signed.append(jnp.where(at < edge, 1.0, -1.0).astype(jnp.bfloat16))
    for parity, pairs in enumerate(lower_pairs(blocks)):

        @pl.when((lane & 1) == parity)
        def _():
            place = 0
            for i in sorted({pair[0] for pair in pairs}):
                picks = [pair[1] for pair in pairs if pair[0] == i]
                columns = slice(picks[0] * block, (picks[-1] + 1) * block)
                total = 0.0
                for sign, piece in zip(signed, pieces):
                    total = total + lax.dot_general(
                        piece[:, i * block : (i + 1) * block] * sign,
                        piece[:, columns],
                        (((0,), (0,)), ((), ())),
                        preferred_element_type=jnp.float32,
                    )
                for index in range(len(picks)):
                    part = total[:, index * block : (index + 1) * block]
                    lower_ref[place] = old_ref[place] + part
                    place += 1


def lower_only(blocks, edge, bits, old, pieces):
    vmem = pl.BlockSpec(memory_space=pltpu.VMEM)
    return pl.pallas_call(
        functools.partial(lower_kernel, blocks, edge, bits),
        in_specs=[vmem] * (1 + len(pieces)),
        out_specs=vmem,
        out_shape=jax.ShapeDtypeStruct(old.shape, jnp.float32),
        input_output_aliases={0: 0},
        name="lower",
    )(*near([old, *pieces]))


def accumulate_kernel(table, blocks, fresh, final, coeffs_ref, earlier_ref, *refs):
    pieces, refs = list(refs[:GROUP]), list(refs[GROUP:])
    old_sum_ref = None if fresh else refs.pop(0)
    old_lower_ref = None if fresh or final else refs.pop(0)
    sum_ref = refs.pop(0)
    lower_ref = None if final else refs.pop(0)
    held_ref, main_ref, sems = refs
    line, lane = seat()
    source = look_up(table, line)
    tile = main_ref.shape[0] // TILES
    depths = [ref.shape[1] // len(table) for ref in (coeffs_ref, earlier_ref)]
    holds = hold_copies(lane, pieces, held_ref, sems)
    loads = []
    for step in range(TILES):
        rows_at = pl.ds(step * tile, tile)
        place = 0
        for side, (ref, depth) in enumerate(zip((coeffs_ref, earlier_ref), depths)):
            base = pl.multiple_of(source * depth, LANES)
            loads.append(
                pltpu.make_async_copy(
                    ref.at[rows_at, pl.ds(base, depth)],
                    main_ref.at[rows_at, pl.ds(place, depth)],
                    sems.at[GROUP + 2 * step + side],
                )
            )
            place += depth
    for copy in holds + loads:
        copy.start()
    for copy in holds:
        copy.wait()
    if not final:
        add_lower(blocks, depths[0], lane, held_ref, old_lower_ref, lower_ref)
    for step in range(TILES):
        loads[2 * step].wait()
        loads[2 * step + 1].wait()
        rows_at = slice(step * tile, (step + 1) * tile)
        total = jnp.dot(main_ref[rows_at, :], held_ref[...], preferred_element_type=jnp.float32)
        sum_ref[rows_at, :] = total if fresh else old_sum_ref[rows_at, :] + total


def accumulate(table, blocks, coeffs, earlier, pieces, state, final):
    rows = coeffs.shape[0]
    width, panel = pieces[0].shape
    fresh = state is None
    block = panel // blocks
    shapes = [(rows, panel), (len(lower_pairs(blocks)[0]), block, block)]
    state = [] if fresh else list(state)
    if final:
        shapes, state = shapes[:1], state[:1]
    anywhere = pl.BlockSpec(memory_space=pl.ANY)
    vmem = pl.BlockSpec(memory_space=pltpu.VMEM)
    return pl.pallas_call(
        functools.partial(accumulate_kernel, table, blocks, fresh, final),
        in_specs=[anywhere] * (2 + GROUP) + [vmem] * len(state),
        out_specs=[vmem] * len(shapes),
        scratch_shapes=[
            pltpu.VMEM((width * GROUP, panel), jnp.bfloat16),
            pltpu.VMEM((rows, width * GROUP), jnp.bfloat16),
            pltpu.SemaphoreType.DMA((GROUP + 2 * TILES,)),
        ],
        out_shape=[jax.ShapeDtypeStruct(shape, jnp.float32) for shape in shapes],
        input_output_aliases={2 + GROUP + i: i for i in range(len(state))},
        cost_estimate=pl.CostEstimate(
            flops=2 * rows * panel * width * GROUP,
            bytes_accessed=2 * rows * width * GROUP,
            transcendentals=0,
        ),
        name="accumulate",
    )(coeffs, earlier, *pieces, *state)


def my_rows(capacity, owner_ref, local_ref):
    panel = owner_ref.shape[1]
    below = lax.broadcasted_iota(jnp.int32, (panel, panel), 0)
    across = lax.broadcasted_iota(jnp.int32, (panel, panel), 1)
    turned = owner_ref[...]
    owners = jnp.sum(jnp.where(below == across, turned, 0), axis=1, keepdims=True)
    same = (owners == turned) & (below < across)
    ranks = jnp.sum(jnp.where(same, 1, 0), axis=0, keepdims=True)
    slots = lax.broadcasted_iota(jnp.int32, (capacity, panel), 0)
    wanted = (ranks == slots) & (turned == lax.axis_index("wide"))
    return jnp.sum(jnp.where(wanted, local_ref[...] + 1, 0), axis=1, keepdims=True) - 1


def cut_kernel(hops, lines, owner_ref, local_ref, coeffs_ref, earlier_ref, *refs):
    outs, (main_ref, sems) = refs[:-2], refs[-2:]
    line, lane = seat()
    depths = [ref.shape[1] // lines for ref in (coeffs_ref, earlier_ref)]
    width = sum(depths) // GROUP
    copies = []
    for index, hop in enumerate(hops):
        place = 0
        for side, (ref, depth) in enumerate(zip((coeffs_ref, earlier_ref), depths)):
            base = pl.multiple_of((line ^ hop) * depth, LANES)
            source = ref.at[:, pl.ds(base, depth)]
            target = main_ref.at[index, :, pl.ds(place, depth)]
            copies.append(pltpu.make_async_copy(source, target, sems.at[index, side]))
            place += depth
    for copy in copies:
        copy.start()
    capacity = outs[0].shape[0]
    at = lax.broadcasted_iota(jnp.int32, (capacity, coeffs_ref.shape[0]), 1)
    select = my_rows(capacity, owner_ref, local_ref) == at
    select = jnp.where(select, 1.0, 0.0).astype(jnp.bfloat16)
    for index in range(len(hops)):
        copies[2 * index].wait()
        copies[2 * index + 1].wait()
        rows = jnp.dot(select, main_ref[index], preferred_element_type=jnp.float32)
        rows = jnp.concatenate([rows[:, : depths[0]], -rows[:, depths[0] :]], axis=1)
        rows = rows.astype(jnp.bfloat16)
        parts = [rows[:, i * width : (i + 1) * width] for i in range(GROUP)]
        for case in range(GROUP):

            @pl.when(lane == case)
            def _():
                for i, part in enumerate(parts):
                    outs[index * GROUP + (i ^ case)][...] = part


def cut(hops, lines, capacity, piv_owner, piv_local, coeffs, earlier):
    vmem = pl.BlockSpec(memory_space=pltpu.VMEM)
    anywhere = pl.BlockSpec(memory_space=pl.ANY)
    total = coeffs.shape[1] + earlier.shape[1]
    shape = jax.ShapeDtypeStruct((capacity, total // (lines * GROUP)), jnp.bfloat16)
    return pl.pallas_call(
        functools.partial(cut_kernel, hops, lines),
        in_specs=[vmem, vmem, anywhere, anywhere],
        out_specs=[vmem] * (len(hops) * GROUP),
        out_shape=[shape] * (len(hops) * GROUP),
        scratch_shapes=[
            pltpu.VMEM((len(hops), coeffs.shape[0], total // lines), jnp.bfloat16),
            pltpu.SemaphoreType.DMA((len(hops), 2)),
        ],
        name="cut",
    )(piv_owner.reshape(1, -1), piv_local[None, :], coeffs, earlier)


def choose(line, table, received):
    names = sorted(set(table))
    values = lax.optimization_barrier(tuple(received[name] for name in names))
    result = values[-1]
    for index, name in enumerate(names[:-1]):
        here = False
        for place, entry in enumerate(table):
            if entry == name:
                here = here | (line == place)
        result = jnp.where(here, values[index], result)
    return result


def split(value):
    high = value.astype(jnp.bfloat16)
    return high, (value - high.astype(jnp.float32)).astype(jnp.bfloat16)


def dot_split(left, right):
    left = jnp.concatenate([left[0], left[0], left[1]], axis=1)
    right = jnp.concatenate([right[0], right[1], right[0]], axis=0)
    return jnp.dot(left, right, preferred_element_type=jnp.float32)


def recur_kernel(blocks, partial_ref, mine_ref, other_ref, inv_ref, keep_ref, give_ref):
    block = inv_ref.shape[1]
    odd = (seat()[1] & 1) == 1
    right_side = lax.axis_index("narrow")
    lower = {}
    for parity, pairs in enumerate(lower_pairs(blocks)):
        here = odd if parity else jnp.logical_not(odd)
        for index, pair in enumerate(pairs):
            lower[pair] = jnp.where(here, mine_ref[index], other_ref[index])
    inverse = [split(inv_ref[j]) for j in range(blocks)]

    def stack(parts, axis):
        return tuple(jnp.concatenate(side, axis=axis) for side in zip(*parts))

    def flip(part):
        return tuple(jnp.transpose(side) for side in part)

    factor = {}
    for j in range(blocks - 1):
        rest = jnp.concatenate(
            [lower[i, j] for i in range(j + 1, blocks)], axis=0
        )
        if j:
            left = stack([stack([factor[i, k] for k in range(j)], 1) for i in range(j + 1, blocks)], 0)
            right = stack([flip(factor[j, k]) for k in range(j)], 0)
            rest = rest - dot_split(left, right)
        made = split(dot_split(split(rest), inverse[j]))
        for i in range(j + 1, blocks):
            rows = slice((i - j - 1) * block, (i - j) * block)
            factor[i, j] = (made[0][rows], made[1][rows])
    new = []
    for j in range(blocks):
        rest = partial_ref[:, j * block : (j + 1) * block]
        if j:
            right = stack([flip(factor[j, k]) for k in range(j)], 0)
            rest = rest - dot_split(stack(new, 1), right)
        result = dot_split(split(rest), inverse[j])
        new.append(split(result))
        half = blocks // 2
        mine = right_side == j // half
        place = pl.ds((j % half) * block, block)

        @pl.when(mine)
        def _():
            keep_ref[:, place] = result

        @pl.when(jnp.logical_not(mine))
        def _():
            give_ref[:, place] = result


def recur(index, partial, mine, other, inv_tiles):
    rows, panel = partial.shape
    blocks = inv_tiles.shape[0]
    rows = rows // SENDS
    half = jax.ShapeDtypeStruct((rows, panel // 2), jnp.float32)
    vmem = pl.BlockSpec(memory_space=pltpu.VMEM)
    return pl.pallas_call(
        functools.partial(recur_kernel, blocks),
        grid=(1,),
        in_specs=[pl.BlockSpec((rows, panel), lambda i: (index, 0)), vmem, vmem, vmem],
        out_specs=[vmem, vmem],
        out_shape=[half, half],
        name="recur",
    )(partial, mine, other, inv_tiles)


def finish_kernel(keep_ref, taken_ref, *refs):
    refs[-1][...] = keep_ref[...] + taken_ref[...]


def finish(index, keep, taken, result):
    rows, columns = keep.shape
    vmem = pl.BlockSpec(memory_space=pltpu.VMEM)
    anywhere = pl.BlockSpec(memory_space=pl.ANY)
    old = [] if result is None else [result]
    return pl.pallas_call(
        finish_kernel,
        grid=(1,),
        in_specs=[vmem, vmem] + [anywhere] * len(old),
        out_specs=pl.BlockSpec((rows, columns), lambda i: (index, 0)),
        out_shape=jax.ShapeDtypeStruct((rows * SENDS, columns), jnp.float32),
        input_output_aliases={2: 0} if old else {},
        name="finish",
    )(*near([keep, taken]), *old)


def lined(*args):
    return lined_panel(*args)


def lined_panel(coeffs, earlier, inv_tiles, piv_local, piv_owner):
    size = lax.axis_size("wide")
    lines = size // GROUP
    me = lax.axis_index("wide")
    line = me // GROUP
    panel = piv_local.shape[0]
    blocks = inv_tiles.shape[0]
    capacity = 3 * panel // size
    widths = [source.shape[1] // size for source in (coeffs, earlier)]
    edge = GROUP * widths[0]

    owners = piv_owner[:, 0]
    positions = jnp.arange(panel, dtype=jnp.int32)
    earlier_same = (owners[:, None] == owners[None, :]) & (positions[None, :] < positions[:, None])
    ranks = jnp.sum(earlier_same, axis=1, dtype=jnp.int32)
    hops = tuple(range(lines - 1, -1, -1))
    cuts = (hops,) if ONE_CUT else (hops[: lines // 2], hops[lines // 2 :])
    parts = {}
    for hops in cuts:
        made = cut(hops, lines, capacity, piv_owner, piv_local, coeffs, earlier)
        for index, hop in enumerate(hops):
            for bit in range(GROUP):
                parts[hop * GROUP + bit] = made[index * GROUP + bit]
    got = []
    for bit in range(size):
        got.append(exchange(parts[bit], "wide", bit, size) if bit else parts[bit])
    stacked = jnp.concatenate(got, axis=0)
    places = (owners ^ me) * capacity + ranks
    taken = places[:, None] == jnp.arange(size * capacity, dtype=jnp.int32)[None, :]
    own = lax.dot_general(
        stacked,
        taken.astype(jnp.bfloat16),
        (((0,), (1,)), ((), ())),
        preferred_element_type=jnp.float32,
    ).astype(jnp.bfloat16)

    up, down = own, own
    tables = arrival_order(lines)
    received = {}
    pieces = [own]
    sources = [tuple(range(lines))]
    for hop in range(1, lines):
        rising = [(i, i + GROUP) for i in range(size - GROUP) if i // GROUP >= hop - 1]
        falling = [(i, i - GROUP) for i in range(GROUP, size) if lines - 1 - i // GROUP >= hop - 1]
        down = lax.ppermute(down, "wide", rising)
        up = lax.ppermute(up, "wide", falling)
        received[("down", hop)] = down
        received[("up", hop)] = up
        pieces.append(choose(line, [tables[i][hop - 1][:2] for i in range(lines)], received))
        sources.append(tuple(tables[i][hop - 1][2] for i in range(lines)))

    groups = []
    for piece in pieces:
        across = exchange(piece, "wide", 2, size)
        beside = exchange(piece, "wide", 1, size)
        corner = exchange(across, "wide", 1, size)
        groups.append([piece, beside, across, corner])
    state = None
    for index, (source, group) in enumerate(zip(sources, groups)):
        final = index == lines - 1
        if final:
            mine = lower_only(blocks, edge, (0, 1), state[1], group[:2])
            mine = lower_only(blocks, edge, (2, 3), mine, group[2:])
        state = accumulate(source, blocks, coeffs, earlier, group, state, final)
    mine = mine + exchange(mine, "narrow", 1, 2)
    other = exchange(mine, "wide", 1, size)
    result = None
    for index in range(SENDS):
        keep, give = recur(index, state[0], mine, other, inv_tiles)
        taken = exchange(give, "narrow", 1, 2)
        result = finish(index, keep, taken, result)
    return result


def on_device(coeffs, earlier, inv_tiles, piv_local, piv_owner):
    chosen = lined if fits(coeffs, earlier, inv_tiles) else general
    return chosen(coeffs, earlier, inv_tiles, piv_local, piv_owner)


def fits(coeffs, earlier, inv_tiles):
    size = lax.axis_size("wide")
    lines = size // GROUP
    return (
        size == lines * GROUP
        and size & (size - 1) == 0
        and lines > 1
        and lax.axis_size("narrow") == 2
        and coeffs.shape[0] % (SUBLANES * TILES) == 0
        and coeffs.shape[1] % (lines * LANES) == 0
        and earlier.shape[1] % (lines * LANES) == 0
        and (coeffs.shape[1] + earlier.shape[1]) % (size * SUBLANES) == 0
        and inv_tiles.shape[0] % 4 == 0
    )


def solution(mesh):
    return jax.shard_map(
        on_device,
        mesh=mesh,
        in_specs=(P("wide", "narrow"), P("wide", "narrow"), P(), P(), P()),
        out_specs=P("wide", "narrow"),
        check_vma=False,
    )
```

```python
import functools

import jax
import jax.numpy as jnp
from jax import lax
from jax.experimental import pallas as pl
from jax.experimental.pallas import tpu as pltpu
from jax.sharding import PartitionSpec as P


LANES = 128
SUBLANES = 16
GROUP = 4
ONE_CUT = True
SENDS = 2
TILES = 2
EXACT = lax.Precision.HIGHEST


def panel_factor(density, diag_block, inv_tiles):
    block_size = inv_tiles.shape[1]
    piv_parts = []
    new_parts = []
    for block_index in range(inv_tiles.shape[0]):
        low_edge = block_index * block_size
        high_edge = low_edge + block_size
        piv_rest = diag_block[:, low_edge:high_edge]
        new_rest = density[:, low_edge:high_edge]
        if block_index > 0:
            piv_left = jnp.concatenate(piv_parts, axis=1)
            new_left = jnp.concatenate(new_parts, axis=1)
            coupling = piv_left[low_edge:high_edge]
            piv_rest = piv_rest - jnp.dot(piv_left, coupling.T, precision=EXACT)
            new_rest = new_rest - jnp.dot(new_left, coupling.T, precision=EXACT)
        piv_parts.append(jnp.dot(piv_rest, inv_tiles[block_index], precision=EXACT))
        new_parts.append(jnp.dot(new_rest, inv_tiles[block_index], precision=EXACT))
    return jnp.concatenate(new_parts, axis=1)


def general(coeffs, earlier, inv_tiles, piv_local, piv_owner):
    owners = piv_owner[:, 0]
    panel_width = piv_local.shape[0]
    mine = owners == lax.axis_index("wide")
    capacity = 3 * panel_width // lax.axis_size("wide")
    positions = jnp.arange(panel_width, dtype=jnp.int32)
    same_owner = owners[:, None] == owners[None, :]
    before = positions[None, :] < positions[:, None]
    slot_rank = jnp.sum(same_owner & before, axis=1)
    slot_index = owners * capacity + slot_rank
    wanted = mine[None, :] & (slot_rank[None, :] == jnp.arange(capacity, dtype=jnp.int32)[:, None])
    local_rows = jnp.sum(jnp.where(wanted, piv_local[None, :], 0), axis=1)
    filled = jnp.any(wanted, axis=1)
    slots = [jnp.where(filled[:, None], source[local_rows], 0) for source in (coeffs, earlier)]
    pieces = [lax.all_gather(slot, "wide", axis=0, tiled=True) for slot in slots]
    select = slot_index[:, None] == jnp.arange(pieces[0].shape[0], dtype=jnp.int32)[None, :]
    select = select.astype(jnp.bfloat16)
    pivots = [
        jnp.dot(select, piece, preferred_element_type=jnp.float32).astype(jnp.bfloat16)
        for piece in pieces
    ]
    partial = [
        jnp.einsum("ro,po->rp", source, pivot, preferred_element_type=jnp.float32)
        for source, pivot in zip((coeffs, earlier), pivots)
    ]
    density = lax.psum_scatter(
        partial[0] - partial[1], "narrow", scatter_dimension=0, tiled=True
    )
    diag = [
        jnp.einsum("qo,po->qp", pivot, pivot, preferred_element_type=jnp.float32)
        for pivot in pivots
    ]
    diag_block = lax.psum(diag[0] - diag[1], "narrow")
    factor = panel_factor(density, diag_block, inv_tiles)
    return lax.all_to_all(factor, "narrow", split_axis=1, concat_axis=0, tiled=True)


def arrival_order(lines):
    tables = []
    for line in range(lines):
        order = []
        for hop in range(1, lines):
            sides = ("up", "down") if 2 * line < lines else ("down", "up")
            for side in sides:
                source = line + hop if side == "up" else line - hop
                if 0 <= source < lines:
                    order.append((side, hop, source))
        tables.append(order)
    return tables


def look_up(table, line):
    result = jnp.int32(table[-1])
    for index, entry in enumerate(table[:-1]):
        result = jnp.where(line == index, jnp.int32(entry), result)
    return result


def exchange(value, axis, bit, size):
    return lax.ppermute(value, axis, [(i, i ^ bit) for i in range(size)])


def lower_pairs(blocks):
    pairs = [(i, j) for i in range(blocks) for j in range(i)]
    half = len(pairs) // 2
    return pairs[:half], pairs[half:]


def near(values):
    return [pltpu.with_memory_space_constraint(value, pltpu.VMEM) for value in values]


def away(values):
    return [pltpu.with_memory_space_constraint(value, pltpu.HBM) for value in values]


def seat():
    me = lax.axis_index("wide")
    return lax.div(me, GROUP), lax.rem(me, GROUP)


def hold_copies(lane, pieces, held_ref, sems):
    width = pieces[0].shape[0]
    copies = []
    for index, piece in enumerate(pieces):
        start = pl.multiple_of((lane ^ index) * width, SUBLANES)
        target = held_ref.at[pl.ds(start, width), :]
        copies.append(pltpu.make_async_copy(piece, target, sems.at[index]))
    return copies


def add_lower(blocks, edge, lane, held_ref, old_ref, lower_ref):
    block = held_ref.shape[1] // blocks
    for parity, pairs in enumerate(lower_pairs(blocks)):

        @pl.when((lane & 1) == parity)
        def _():
            place = 0
            for i in sorted({pair[0] for pair in pairs}):
                picks = [pair[1] for pair in pairs if pair[0] == i]
                rows = slice(i * block, (i + 1) * block)
                columns = slice(picks[0] * block, (picks[-1] + 1) * block)
                terms = [
                    lax.dot_general(
                        held_ref[part, rows],
                        held_ref[part, columns],
                        (((0,), (0,)), ((), ())),
                        preferred_element_type=jnp.float32,
                    )
                    for part in (slice(0, edge), slice(edge, held_ref.shape[0]))
                ]
                total = terms[0] - terms[1]
                for index in range(len(picks)):
                    part = total[:, index * block : (index + 1) * block]
                    if old_ref is not None:
                        part = old_ref[place] + part
                    lower_ref[place] = part
                    place += 1


def lower_kernel(blocks, edge, bits, old_ref, *refs):
    pieces, lower_ref = refs[:-1], refs[-1]
    _, lane = seat()
    width, panel = pieces[0].shape
    block = panel // blocks
    signed = []
    for bit, piece in zip(bits, pieces):
        at = (lane ^ bit) * width + lax.broadcasted_iota(jnp.int32, (width, block), 0)
        signed.append(jnp.where(at < edge, 1.0, -1.0).astype(jnp.bfloat16))
    for parity, pairs in enumerate(lower_pairs(blocks)):

        @pl.when((lane & 1) == parity)
        def _():
            place = 0
            for i in sorted({pair[0] for pair in pairs}):
                picks = [pair[1] for pair in pairs if pair[0] == i]
                columns = slice(picks[0] * block, (picks[-1] + 1) * block)
                total = 0.0
                for sign, piece in zip(signed, pieces):
                    total = total + lax.dot_general(
                        piece[:, i * block : (i + 1) * block] * sign,
                        piece[:, columns],
                        (((0,), (0,)), ((), ())),
                        preferred_element_type=jnp.float32,
                    )
                for index in range(len(picks)):
                    part = total[:, index * block : (index + 1) * block]
                    lower_ref[place] = old_ref[place] + part
                    place += 1


def lower_only(blocks, edge, bits, old, pieces):
    vmem = pl.BlockSpec(memory_space=pltpu.VMEM)
    return pl.pallas_call(
        functools.partial(lower_kernel, blocks, edge, bits),
        in_specs=[vmem] * (1 + len(pieces)),
        out_specs=vmem,
        out_shape=jax.ShapeDtypeStruct(old.shape, jnp.float32),
        input_output_aliases={0: 0},
        compiler_params=pltpu.CompilerParams(vmem_limit_bytes=8 << 20),
        name="lower",
    )(*near([old, *pieces]))


def accumulate_kernel(table, blocks, fresh, final, tick_ref, coeffs_ref, earlier_ref, *refs):
    pieces, refs = list(refs[:GROUP]), list(refs[GROUP:])
    old_sum_ref = None if fresh else refs.pop(0)
    old_lower_ref = None if fresh or final else refs.pop(0)
    sum_ref = refs.pop(0)
    lower_ref = None if final else refs.pop(0)
    held_ref, main_ref, sems = refs
    line, lane = seat()
    source = look_up(table, line)
    tile = main_ref.shape[0] // TILES
    depths = [ref.shape[1] // len(table) for ref in (coeffs_ref, earlier_ref)]
    holds = hold_copies(lane, pieces, held_ref, sems)
    loads = []
    for step in range(TILES):
        rows_at = pl.ds(step * tile, tile)
        place = 0
        for side, (ref, depth) in enumerate(zip((coeffs_ref, earlier_ref), depths)):
            base = pl.multiple_of(source * depth, LANES)
            loads.append(
                pltpu.make_async_copy(
                    ref.at[rows_at, pl.ds(base, depth)],
                    main_ref.at[rows_at, pl.ds(place, depth)],
                    sems.at[GROUP + 2 * step + side],
                )
            )
            place += depth
    for copy in holds + loads:
        copy.start()
    for copy in holds:
        copy.wait()
    if not final:
        add_lower(blocks, depths[0], lane, held_ref, old_lower_ref, lower_ref)
    for step in range(TILES):
        loads[2 * step].wait()
        loads[2 * step + 1].wait()
        rows_at = slice(step * tile, (step + 1) * tile)
        total = jnp.dot(main_ref[rows_at, :], held_ref[...], preferred_element_type=jnp.float32)
        sum_ref[rows_at, :] = total if fresh else old_sum_ref[rows_at, :] + total


def accumulate(table, blocks, ticked, coeffs, earlier, pieces, state, final):
    rows = coeffs.shape[0]
    width, panel = pieces[0].shape
    fresh = state is None
    block = panel // blocks
    shapes = [(rows, panel), (len(lower_pairs(blocks)[0]), block, block)]
    state = [] if fresh else list(state)
    if final:
        shapes, state = shapes[:1], state[:1]
    anywhere = pl.BlockSpec(memory_space=pl.ANY)
    vmem = pl.BlockSpec(memory_space=pltpu.VMEM)
    return pl.pallas_call(
        functools.partial(accumulate_kernel, table, blocks, fresh, final),
        in_specs=[pl.BlockSpec(memory_space=pltpu.SMEM)]
        + [anywhere] * 2
        + [vmem] * (GROUP + len(state)),
        out_specs=[vmem] * len(shapes),
        scratch_shapes=[
            pltpu.VMEM((width * GROUP, panel), jnp.bfloat16),
            pltpu.VMEM((rows, width * GROUP), jnp.bfloat16),
            pltpu.SemaphoreType.DMA((GROUP + 2 * TILES,)),
        ],
        out_shape=[jax.ShapeDtypeStruct(shape, jnp.float32) for shape in shapes],
        input_output_aliases={3 + GROUP + i: i for i in range(len(state))},
        cost_estimate=pl.CostEstimate(
            flops=2 * rows * panel * width * GROUP,
            bytes_accessed=2 * rows * width * GROUP,
            transcendentals=0,
        ),
        compiler_params=pltpu.CompilerParams(vmem_limit_bytes=16 << 20),
        name="accumulate",
    )(ticked, *away([coeffs, earlier]), *near([*pieces, *state]))


def my_rows(capacity, owner_ref, local_ref):
    panel = owner_ref.shape[1]
    below = lax.broadcasted_iota(jnp.int32, (panel, panel), 0)
    across = lax.broadcasted_iota(jnp.int32, (panel, panel), 1)
    turned = owner_ref[...]
    owners = jnp.sum(jnp.where(below == across, turned, 0), axis=1, keepdims=True)
    same = (owners == turned) & (below < across)
    ranks = jnp.sum(jnp.where(same, 1, 0), axis=0, keepdims=True)
    slots = lax.broadcasted_iota(jnp.int32, (capacity, panel), 0)
    wanted = (ranks == slots) & (turned == lax.axis_index("wide"))
    return jnp.sum(jnp.where(wanted, local_ref[...] + 1, 0), axis=1, keepdims=True) - 1


def cut_kernel(hops, lines, owner_ref, local_ref, coeffs_ref, earlier_ref, *refs):
    outs, (main_ref, sems) = refs[:-2], refs[-2:]
    line, lane = seat()
    depths = [ref.shape[1] // lines for ref in (coeffs_ref, earlier_ref)]
    width = sum(depths) // GROUP
    copies = []
    for index, hop in enumerate(hops):
        place = 0
        for side, (ref, depth) in enumerate(zip((coeffs_ref, earlier_ref), depths)):
            base = pl.multiple_of((line ^ hop) * depth, LANES)
            source = ref.at[:, pl.ds(base, depth)]
            target = main_ref.at[index, :, pl.ds(place, depth)]
            copies.append(pltpu.make_async_copy(source, target, sems.at[index, side]))
            place += depth
    for copy in copies:
        copy.start()
    capacity = outs[0].shape[0]
    at = lax.broadcasted_iota(jnp.int32, (capacity, coeffs_ref.shape[0]), 1)
    select = my_rows(capacity, owner_ref, local_ref) == at
    select = jnp.where(select, 1.0, 0.0).astype(jnp.bfloat16)
    for index in range(len(hops)):
        copies[2 * index].wait()
        copies[2 * index + 1].wait()
        rows = jnp.dot(select, main_ref[index], preferred_element_type=jnp.float32)
        rows = jnp.concatenate([rows[:, : depths[0]], -rows[:, depths[0] :]], axis=1)
        rows = rows.astype(jnp.bfloat16)
        parts = [rows[:, i * width : (i + 1) * width] for i in range(GROUP)]
        for case in range(GROUP):

            @pl.when(lane == case)
            def _():
                for i, part in enumerate(parts):
                    outs[index * GROUP + (i ^ case)][...] = part


def cut(hops, lines, capacity, piv_owner, piv_local, coeffs, earlier):
    vmem = pl.BlockSpec(memory_space=pltpu.VMEM)
    anywhere = pl.BlockSpec(memory_space=pl.ANY)
    total = coeffs.shape[1] + earlier.shape[1]
    shape = jax.ShapeDtypeStruct((capacity, total // (lines * GROUP)), jnp.bfloat16)
    return pl.pallas_call(
        functools.partial(cut_kernel, hops, lines),
        in_specs=[vmem, vmem, anywhere, anywhere],
        out_specs=[vmem] * (len(hops) * GROUP),
        out_shape=[shape] * (len(hops) * GROUP),
        scratch_shapes=[
            pltpu.VMEM((len(hops), coeffs.shape[0], total // lines), jnp.bfloat16),
            pltpu.SemaphoreType.DMA((len(hops), 2)),
        ],
        compiler_params=pltpu.CompilerParams(vmem_limit_bytes=24 << 20),
        name="cut",
    )(piv_owner.reshape(1, -1), piv_local[None, :], *away([coeffs, earlier]))


def tick_kernel(local_ref, out_ref):
    out_ref[0, 0] = local_ref[0, 0]


def tick(local):
    smem = pl.BlockSpec(memory_space=pltpu.SMEM)
    return pl.pallas_call(
        tick_kernel,
        in_specs=[smem],
        out_specs=smem,
        out_shape=jax.ShapeDtypeStruct((1, 1), jnp.int32),
    )(local)


def choose(line, table, received):
    names = sorted(set(table))
    values = lax.optimization_barrier(tuple(received[name] for name in names))
    result = values[-1]
    for index, name in enumerate(names[:-1]):
        here = False
        for place, entry in enumerate(table):
            if entry == name:
                here = here | (line == place)
        result = jnp.where(here, values[index], result)
    return result


def split(value):
    high = value.astype(jnp.bfloat16)
    return high, (value - high.astype(jnp.float32)).astype(jnp.bfloat16)


def dot_split(left, right):
    left = jnp.concatenate([left[0], left[0], left[1]], axis=1)
    right = jnp.concatenate([right[0], right[1], right[0]], axis=0)
    return jnp.dot(left, right, preferred_element_type=jnp.float32)


def recur_kernel(blocks, partial_ref, mine_ref, other_ref, inv_ref, keep_ref, give_ref):
    block = inv_ref.shape[1]
    odd = (seat()[1] & 1) == 1
    right_side = lax.axis_index("narrow")
    lower = {}
    for parity, pairs in enumerate(lower_pairs(blocks)):
        here = odd if parity else jnp.logical_not(odd)
        for index, pair in enumerate(pairs):
            lower[pair] = jnp.where(here, mine_ref[index], other_ref[index])
    inverse = [split(inv_ref[j]) for j in range(blocks)]

    def stack(parts, axis):
        return tuple(jnp.concatenate(side, axis=axis) for side in zip(*parts))

    def flip(part):
        return tuple(jnp.transpose(side) for side in part)

    factor = {}
    for j in range(blocks - 1):
        rest = jnp.concatenate(
            [lower[i, j] for i in range(j + 1, blocks)], axis=0
        )
        if j:
            left = stack([stack([factor[i, k] for k in range(j)], 1) for i in range(j + 1, blocks)], 0)
            right = stack([flip(factor[j, k]) for k in range(j)], 0)
            rest = rest - dot_split(left, right)
        made = split(dot_split(split(rest), inverse[j]))
        for i in range(j + 1, blocks):
            rows = slice((i - j - 1) * block, (i - j) * block)
            factor[i, j] = (made[0][rows], made[1][rows])
    new = []
    for j in range(blocks):
        rest = partial_ref[:, j * block : (j + 1) * block]
        if j:
            right = stack([flip(factor[j, k]) for k in range(j)], 0)
            rest = rest - dot_split(stack(new, 1), right)
        result = dot_split(split(rest), inverse[j])
        new.append(split(result))
        half = blocks // 2
        mine = right_side == j // half
        place = pl.ds((j % half) * block, block)

        @pl.when(mine)
        def _():
            keep_ref[:, place] = result

        @pl.when(jnp.logical_not(mine))
        def _():
            give_ref[:, place] = result


def recur(index, partial, mine, other, inv_tiles):
    rows, panel = partial.shape
    blocks = inv_tiles.shape[0]
    rows = rows // SENDS
    half = jax.ShapeDtypeStruct((rows, panel // 2), jnp.float32)
    vmem = pl.BlockSpec(memory_space=pltpu.VMEM)
    return pl.pallas_call(
        functools.partial(recur_kernel, blocks),
        grid=(1,),
        in_specs=[pl.BlockSpec((rows, panel), lambda i: (index, 0)), vmem, vmem, vmem],
        out_specs=[vmem, vmem],
        out_shape=[half, half],
        compiler_params=pltpu.CompilerParams(vmem_limit_bytes=20 << 20),
        name="recur",
    )(*near([partial, mine, other]), inv_tiles)


def finish_kernel(keep_ref, taken_ref, *refs):
    refs[-1][...] = keep_ref[...] + taken_ref[...]


def finish(index, keep, taken, result):
    rows, columns = keep.shape
    vmem = pl.BlockSpec(memory_space=pltpu.VMEM)
    anywhere = pl.BlockSpec(memory_space=pl.ANY)
    old = [] if result is None else [result]
    return pl.pallas_call(
        finish_kernel,
        grid=(1,),
        in_specs=[vmem, vmem] + [anywhere] * len(old),
        out_specs=pl.BlockSpec((rows, columns), lambda i: (index, 0)),
        out_shape=jax.ShapeDtypeStruct((rows * SENDS, columns), jnp.float32),
        input_output_aliases={2: 0} if old else {},
        compiler_params=pltpu.CompilerParams(vmem_limit_bytes=8 << 20),
        name="finish",
    )(*near([keep, taken]), *old)


def lined(*args):
    return lined_panel(*args)


def lined_panel(coeffs, earlier, inv_tiles, piv_local, piv_owner):
    size = lax.axis_size("wide")
    lines = size // GROUP
    me = lax.axis_index("wide")
    line = me // GROUP
    panel = piv_local.shape[0]
    blocks = inv_tiles.shape[0]
    capacity = 3 * panel // size
    widths = [source.shape[1] // size for source in (coeffs, earlier)]
    edge = GROUP * widths[0]

    owners = piv_owner[:, 0]
    positions = jnp.arange(panel, dtype=jnp.int32)
    earlier_same = (owners[:, None] == owners[None, :]) & (positions[None, :] < positions[:, None])
    ranks = jnp.sum(earlier_same, axis=1, dtype=jnp.int32)
    hops = tuple(range(lines - 1, -1, -1))
    cuts = (hops,) if ONE_CUT else (hops[: lines // 2], hops[lines // 2 :])
    parts = {}
    for hops in cuts:
        made = cut(hops, lines, capacity, piv_owner, piv_local, coeffs, earlier)
        for index, hop in enumerate(hops):
            for bit in range(GROUP):
                parts[hop * GROUP + bit] = made[index * GROUP + bit]
    got = []
    for bit in range(size):
        got.append(exchange(parts[bit], "wide", bit, size) if bit else parts[bit])
    stacked = jnp.concatenate(got, axis=0)
    places = (owners ^ me) * capacity + ranks
    taken = places[:, None] == jnp.arange(size * capacity, dtype=jnp.int32)[None, :]
    own = lax.dot_general(
        stacked,
        taken.astype(jnp.bfloat16),
        (((0,), (1,)), ((), ())),
        preferred_element_type=jnp.float32,
    ).astype(jnp.bfloat16)

    up, down = own, own
    tables = arrival_order(lines)
    received = {}
    pieces = [own]
    sources = [tuple(range(lines))]
    for hop in range(1, lines):
        rising = [(i, i + GROUP) for i in range(size - GROUP) if i // GROUP >= hop - 1]
        falling = [(i, i - GROUP) for i in range(GROUP, size) if lines - 1 - i // GROUP >= hop - 1]
        down = lax.ppermute(down, "wide", rising)
        up = lax.ppermute(up, "wide", falling)
        received[("down", hop)] = down
        received[("up", hop)] = up
        pieces.append(choose(line, [tables[i][hop - 1][:2] for i in range(lines)], received))
        sources.append(tuple(tables[i][hop - 1][2] for i in range(lines)))

    groups = []
    for piece in pieces:
        across = exchange(piece, "wide", 2, size)
        beside = exchange(piece, "wide", 1, size)
        corner = exchange(across, "wide", 1, size)
        groups.append([piece, beside, across, corner])
    ticks = {hop: tick(piv_local[:1, None]) for hop in range(1, lines - 1)}
    state = None
    for index, (source, group) in enumerate(zip(sources, groups)):
        final = index == lines - 1
        if final:
            mine = lower_only(blocks, edge, (0, 1), state[1], group[:2])
            mine = lower_only(blocks, edge, (2, 3), mine, group[2:])
        ticked = ticks[min(max(index, 1), lines - 2)]
        state = accumulate(source, blocks, ticked, coeffs, earlier, group, state, final)
    mine = mine + exchange(mine, "narrow", 1, 2)
    other = exchange(mine, "wide", 1, size)
    result = None
    for index in range(SENDS):
        keep, give = recur(index, state[0], mine, other, inv_tiles)
        taken = exchange(give, "narrow", 1, 2)
        result = finish(index, keep, taken, result)
    return result


def on_device(coeffs, earlier, inv_tiles, piv_local, piv_owner):
    chosen = lined if fits(coeffs, earlier, inv_tiles) else general
    return chosen(coeffs, earlier, inv_tiles, piv_local, piv_owner)


def fits(coeffs, earlier, inv_tiles):
    size = lax.axis_size("wide")
    lines = size // GROUP
    return (
        size == lines * GROUP
        and size & (size - 1) == 0
        and lines > 1
        and lax.axis_size("narrow") == 2
        and coeffs.shape[0] % (SUBLANES * TILES) == 0
        and coeffs.shape[1] % (lines * LANES) == 0
        and earlier.shape[1] % (lines * LANES) == 0
        and (coeffs.shape[1] + earlier.shape[1]) % (size * SUBLANES) == 0
        and inv_tiles.shape[0] % 4 == 0
    )


def solution(mesh):
    return jax.shard_map(
        on_device,
        mesh=mesh,
        in_specs=(P("wide", "narrow"), P("wide", "narrow"), P(), P(), P()),
        out_specs=P("wide", "narrow"),
        check_vma=False,
    )
```

```python
import functools

import jax
import jax.numpy as jnp
from jax import lax
from jax.experimental import pallas as pl
from jax.experimental.pallas import tpu as pltpu
from jax.sharding import PartitionSpec as P


LANES = 128
SUBLANES = 16
GROUP = 4
ONE_CUT = True
SENDS = 4
TILES = 2
EXACT = lax.Precision.HIGHEST


def panel_factor(density, diag_block, inv_tiles):
    block_size = inv_tiles.shape[1]
    piv_parts = []
    new_parts = []
    for block_index in range(inv_tiles.shape[0]):
        low_edge = block_index * block_size
        high_edge = low_edge + block_size
        piv_rest = diag_block[:, low_edge:high_edge]
        new_rest = density[:, low_edge:high_edge]
        if block_index > 0:
            piv_left = jnp.concatenate(piv_parts, axis=1)
            new_left = jnp.concatenate(new_parts, axis=1)
            coupling = piv_left[low_edge:high_edge]
            piv_rest = piv_rest - jnp.dot(piv_left, coupling.T, precision=EXACT)
            new_rest = new_rest - jnp.dot(new_left, coupling.T, precision=EXACT)
        piv_parts.append(jnp.dot(piv_rest, inv_tiles[block_index], precision=EXACT))
        new_parts.append(jnp.dot(new_rest, inv_tiles[block_index], precision=EXACT))
    return jnp.concatenate(new_parts, axis=1)


def general(coeffs, earlier, inv_tiles, piv_local, piv_owner):
    owners = piv_owner[:, 0]
    panel_width = piv_local.shape[0]
    mine = owners == lax.axis_index("wide")
    capacity = 3 * panel_width // lax.axis_size("wide")
    positions = jnp.arange(panel_width, dtype=jnp.int32)
    same_owner = owners[:, None] == owners[None, :]
    before = positions[None, :] < positions[:, None]
    slot_rank = jnp.sum(same_owner & before, axis=1)
    slot_index = owners * capacity + slot_rank
    wanted = mine[None, :] & (slot_rank[None, :] == jnp.arange(capacity, dtype=jnp.int32)[:, None])
    local_rows = jnp.sum(jnp.where(wanted, piv_local[None, :], 0), axis=1)
    filled = jnp.any(wanted, axis=1)
    slots = [jnp.where(filled[:, None], source[local_rows], 0) for source in (coeffs, earlier)]
    pieces = [lax.all_gather(slot, "wide", axis=0, tiled=True) for slot in slots]
    select = slot_index[:, None] == jnp.arange(pieces[0].shape[0], dtype=jnp.int32)[None, :]
    select = select.astype(jnp.bfloat16)
    pivots = [
        jnp.dot(select, piece, preferred_element_type=jnp.float32).astype(jnp.bfloat16)
        for piece in pieces
    ]
    partial = [
        jnp.einsum("ro,po->rp", source, pivot, preferred_element_type=jnp.float32)
        for source, pivot in zip((coeffs, earlier), pivots)
    ]
    density = lax.psum_scatter(
        partial[0] - partial[1], "narrow", scatter_dimension=0, tiled=True
    )
    diag = [
        jnp.einsum("qo,po->qp", pivot, pivot, preferred_element_type=jnp.float32)
        for pivot in pivots
    ]
    diag_block = lax.psum(diag[0] - diag[1], "narrow")
    factor = panel_factor(density, diag_block, inv_tiles)
    return lax.all_to_all(factor, "narrow", split_axis=1, concat_axis=0, tiled=True)


def arrival_order(lines):
    tables = []
    for line in range(lines):
        order = []
        for hop in range(1, lines):
            sides = ("up", "down") if 2 * line < lines else ("down", "up")
            for side in sides:
                source = line + hop if side == "up" else line - hop
                if 0 <= source < lines:
                    order.append((side, hop, source))
        tables.append(order)
    return tables


def look_up(table, line):
    result = jnp.int32(table[-1])
    for index, entry in enumerate(table[:-1]):
        result = jnp.where(line == index, jnp.int32(entry), result)
    return result


def exchange(value, axis, bit, size):
    return lax.ppermute(value, axis, [(i, i ^ bit) for i in range(size)])


def lower_pairs(blocks):
    pairs = [(i, j) for i in range(blocks) for j in range(i)]
    half = len(pairs) // 2
    return pairs[:half], pairs[half:]


def near(values):
    return [pltpu.with_memory_space_constraint(value, pltpu.VMEM) for value in values]


def away(values):
    return [pltpu.with_memory_space_constraint(value, pltpu.HBM) for value in values]


def seat():
    me = lax.axis_index("wide")
    return lax.div(me, GROUP), lax.rem(me, GROUP)


def hold_copies(lane, pieces, held_ref, sems):
    width = pieces[0].shape[0]
    copies = []
    for index, piece in enumerate(pieces):
        start = pl.multiple_of((lane ^ index) * width, SUBLANES)
        target = held_ref.at[pl.ds(start, width), :]
        copies.append(pltpu.make_async_copy(piece, target, sems.at[index]))
    return copies


def add_lower(blocks, edge, lane, held_ref, old_ref, lower_ref):
    block = held_ref.shape[1] // blocks
    for parity, pairs in enumerate(lower_pairs(blocks)):

        @pl.when((lane & 1) == parity)
        def _():
            place = 0
            for i in sorted({pair[0] for pair in pairs}):
                picks = [pair[1] for pair in pairs if pair[0] == i]
                rows = slice(i * block, (i + 1) * block)
                columns = slice(picks[0] * block, (picks[-1] + 1) * block)
                terms = [
                    lax.dot_general(
                        held_ref[part, rows],
                        held_ref[part, columns],
                        (((0,), (0,)), ((), ())),
                        preferred_element_type=jnp.float32,
                    )
                    for part in (slice(0, edge), slice(edge, held_ref.shape[0]))
                ]
                total = terms[0] - terms[1]
                for index in range(len(picks)):
                    part = total[:, index * block : (index + 1) * block]
                    if old_ref is not None:
                        part = old_ref[place] + part
                    lower_ref[place] = part
                    place += 1


def lower_kernel(blocks, edge, bits, old_ref, *refs):
    pieces, lower_ref = refs[:-1], refs[-1]
    _, lane = seat()
    width, panel = pieces[0].shape
    block = panel // blocks
    signed = []
    for bit, piece in zip(bits, pieces):
        at = (lane ^ bit) * width + lax.broadcasted_iota(jnp.int32, (width, block), 0)
        signed.append(jnp.where(at < edge, 1.0, -1.0).astype(jnp.bfloat16))
    for parity, pairs in enumerate(lower_pairs(blocks)):

        @pl.when((lane & 1) == parity)
        def _():
            place = 0
            for i in sorted({pair[0] for pair in pairs}):
                picks = [pair[1] for pair in pairs if pair[0] == i]
                columns = slice(picks[0] * block, (picks[-1] + 1) * block)
                total = 0.0
                for sign, piece in zip(signed, pieces):
                    total = total + lax.dot_general(
                        piece[:, i * block : (i + 1) * block] * sign,
                        piece[:, columns],
                        (((0,), (0,)), ((), ())),
                        preferred_element_type=jnp.float32,
                    )
                for index in range(len(picks)):
                    part = total[:, index * block : (index + 1) * block]
                    lower_ref[place] = old_ref[place] + part
                    place += 1


def lower_only(blocks, edge, bits, old, pieces):
    vmem = pl.BlockSpec(memory_space=pltpu.VMEM)
    return pl.pallas_call(
        functools.partial(lower_kernel, blocks, edge, bits),
        in_specs=[vmem] * (1 + len(pieces)),
        out_specs=vmem,
        out_shape=jax.ShapeDtypeStruct(old.shape, jnp.float32),
        input_output_aliases={0: 0},
        compiler_params=pltpu.CompilerParams(vmem_limit_bytes=8 << 20),
        name="lower",
    )(*near([old, *pieces]))


def accumulate_kernel(table, blocks, fresh, final, tick_ref, coeffs_ref, earlier_ref, *refs):
    pieces, refs = list(refs[:GROUP]), list(refs[GROUP:])
    old_sum_ref = None if fresh else refs.pop(0)
    old_lower_ref = None if fresh or final else refs.pop(0)
    sum_ref = refs.pop(0)
    lower_ref = None if final else refs.pop(0)
    held_ref, main_ref, sems = refs
    line, lane = seat()
    source = look_up(table, line)
    tile = main_ref.shape[0] // TILES
    depths = [ref.shape[1] // len(table) for ref in (coeffs_ref, earlier_ref)]
    holds = hold_copies(lane, pieces, held_ref, sems)
    loads = []
    for step in range(TILES):
        rows_at = pl.ds(step * tile, tile)
        place = 0
        for side, (ref, depth) in enumerate(zip((coeffs_ref, earlier_ref), depths)):
            base = pl.multiple_of(source * depth, LANES)
            loads.append(
                pltpu.make_async_copy(
                    ref.at[rows_at, pl.ds(base, depth)],
                    main_ref.at[rows_at, pl.ds(place, depth)],
                    sems.at[GROUP + 2 * step + side],
                )
            )
            place += depth
    for copy in holds + loads:
        copy.start()
    for copy in holds:
        copy.wait()
    if not final:
        add_lower(blocks, depths[0], lane, held_ref, old_lower_ref, lower_ref)
    for step in range(TILES):
        loads[2 * step].wait()
        loads[2 * step + 1].wait()
        rows_at = slice(step * tile, (step + 1) * tile)
        total = jnp.dot(main_ref[rows_at, :], held_ref[...], preferred_element_type=jnp.float32)
        sum_ref[rows_at, :] = total if fresh else old_sum_ref[rows_at, :] + total


def accumulate(table, blocks, ticked, coeffs, earlier, pieces, state, final):
    rows = coeffs.shape[0]
    width, panel = pieces[0].shape
    fresh = state is None
    block = panel // blocks
    shapes = [(rows, panel), (len(lower_pairs(blocks)[0]), block, block)]
    state = [] if fresh else list(state)
    if final:
        shapes, state = shapes[:1], state[:1]
    anywhere = pl.BlockSpec(memory_space=pl.ANY)
    vmem = pl.BlockSpec(memory_space=pltpu.VMEM)
    return pl.pallas_call(
        functools.partial(accumulate_kernel, table, blocks, fresh, final),
        in_specs=[anywhere] * 3
        + [vmem] * (GROUP + len(state)),
        out_specs=[vmem] * len(shapes),
        scratch_shapes=[
            pltpu.VMEM((width * GROUP, panel), jnp.bfloat16),
            pltpu.VMEM((rows, width * GROUP), jnp.bfloat16),
            pltpu.SemaphoreType.DMA((GROUP + 2 * TILES,)),
        ],
        out_shape=[jax.ShapeDtypeStruct(shape, jnp.float32) for shape in shapes],
        input_output_aliases={3 + GROUP + i: i for i in range(len(state))},
        cost_estimate=pl.CostEstimate(
            flops=2 * rows * panel * width * GROUP,
            bytes_accessed=2 * rows * width * GROUP,
            transcendentals=0,
        ),
        compiler_params=pltpu.CompilerParams(vmem_limit_bytes=16 << 20),
        name="accumulate",
    )(ticked, *away([coeffs, earlier]), *near([*pieces, *state]))


def my_rows(capacity, pivot_ref):
    panel = pivot_ref.shape[1]
    below = lax.broadcasted_iota(jnp.int32, (panel, panel), 0)
    across = lax.broadcasted_iota(jnp.int32, (panel, panel), 1)
    turned = pivot_ref[0:1, :]
    owners = jnp.sum(jnp.where(below == across, turned, 0), axis=1, keepdims=True)
    same = (owners == turned) & (below < across)
    ranks = jnp.sum(jnp.where(same, 1, 0), axis=0, keepdims=True)
    slots = lax.broadcasted_iota(jnp.int32, (capacity, panel), 0)
    wanted = (ranks == slots) & (turned == lax.axis_index("wide"))
    return jnp.sum(jnp.where(wanted, pivot_ref[1:2, :] + 1, 0), axis=1, keepdims=True) - 1


def cut_kernel(hops, lines, pivot_ref, coeffs_ref, earlier_ref, *refs):
    outs, (main_ref, sems) = refs[:-2], refs[-2:]
    line, lane = seat()
    depths = [ref.shape[1] // lines for ref in (coeffs_ref, earlier_ref)]
    width = sum(depths) // GROUP
    copies = []
    for index, hop in enumerate(hops):
        place = 0
        for side, (ref, depth) in enumerate(zip((coeffs_ref, earlier_ref), depths)):
            base = pl.multiple_of((line ^ hop) * depth, LANES)
            source = ref.at[:, pl.ds(base, depth)]
            target = main_ref.at[index, :, pl.ds(place, depth)]
            copies.append(pltpu.make_async_copy(source, target, sems.at[index, side]))
            place += depth
    for copy in copies:
        copy.start()
    capacity = outs[0].shape[0]
    at = lax.broadcasted_iota(jnp.int32, (capacity, coeffs_ref.shape[0]), 1)
    select = my_rows(capacity, pivot_ref) == at
    select = jnp.where(select, 1.0, 0.0).astype(jnp.bfloat16)
    for index in range(len(hops)):
        copies[2 * index].wait()
        copies[2 * index + 1].wait()
        rows = jnp.dot(select, main_ref[index], preferred_element_type=jnp.float32)
        rows = jnp.concatenate([rows[:, : depths[0]], -rows[:, depths[0] :]], axis=1)
        rows = rows.astype(jnp.bfloat16)
        parts = [rows[:, i * width : (i + 1) * width] for i in range(GROUP)]
        for case in range(GROUP):

            @pl.when(lane == case)
            def _():
                for i, part in enumerate(parts):
                    outs[index * GROUP + (i ^ case)][...] = part


def cut(hops, lines, capacity, piv_owner, piv_local, coeffs, earlier):
    vmem = pl.BlockSpec(memory_space=pltpu.VMEM)
    anywhere = pl.BlockSpec(memory_space=pl.ANY)
    total = coeffs.shape[1] + earlier.shape[1]
    pivots = jnp.concatenate([piv_owner.reshape(1, -1), piv_local[None, :]], axis=0)
    pivots = near([pivots])[0]
    shape = jax.ShapeDtypeStruct((capacity, total // (lines * GROUP)), jnp.bfloat16)
    return pl.pallas_call(
        functools.partial(cut_kernel, hops, lines),
        in_specs=[vmem, anywhere, anywhere],
        out_specs=[vmem] * (len(hops) * GROUP),
        out_shape=[shape] * (len(hops) * GROUP),
        scratch_shapes=[
            pltpu.VMEM((len(hops), coeffs.shape[0], total // lines), jnp.bfloat16),
            pltpu.SemaphoreType.DMA((len(hops), 2)),
        ],
        compiler_params=pltpu.CompilerParams(vmem_limit_bytes=24 << 20),
        name="cut",
    )(pivots, *away([coeffs, earlier]))


def tick(local, hop):
    return local * (hop + 2) + hop


def choose_kernel(order, *refs):
    which = look_up(order, seat()[0])
    for index, source in enumerate(refs[:-1]):

        @pl.when(which == index)
        def _():
            refs[-1][...] = source[...]


def choose(table, received):
    names = sorted(set(table))
    vmem = pl.BlockSpec(memory_space=pltpu.VMEM)
    sources = [received[name] for name in names]
    return pl.pallas_call(
        functools.partial(choose_kernel, tuple(names.index(name) for name in table)),
        in_specs=[vmem] * len(names),
        out_specs=vmem,
        out_shape=jax.ShapeDtypeStruct(sources[0].shape, sources[0].dtype),
        compiler_params=pltpu.CompilerParams(vmem_limit_bytes=4 << 20),
        name="choose",
    )(*near(sources))


def split(value):
    high = value.astype(jnp.bfloat16)
    return high, (value - high.astype(jnp.float32)).astype(jnp.bfloat16)


def dot_split(left, right):
    left = jnp.concatenate([left[0], left[0], left[1]], axis=1)
    right = jnp.concatenate([right[0], right[1], right[0]], axis=0)
    return jnp.dot(left, right, preferred_element_type=jnp.float32)


def recur_kernel(blocks, partial_ref, mine_ref, other_ref, inv_ref, keep_ref, give_ref):
    block = inv_ref.shape[1]
    odd = (seat()[1] & 1) == 1
    right_side = lax.axis_index("narrow")
    lower = {}
    for parity, pairs in enumerate(lower_pairs(blocks)):
        here = odd if parity else jnp.logical_not(odd)
        for index, pair in enumerate(pairs):
            lower[pair] = jnp.where(here, mine_ref[index], other_ref[index])
    inverse = [split(inv_ref[j]) for j in range(blocks)]

    def stack(parts, axis):
        return tuple(jnp.concatenate(side, axis=axis) for side in zip(*parts))

    def flip(part):
        return tuple(jnp.transpose(side) for side in part)

    factor = {}
    for j in range(blocks - 1):
        rest = jnp.concatenate(
            [lower[i, j] for i in range(j + 1, blocks)], axis=0
        )
        if j:
            left = stack([stack([factor[i, k] for k in range(j)], 1) for i in range(j + 1, blocks)], 0)
            right = stack([flip(factor[j, k]) for k in range(j)], 0)
            rest = rest - dot_split(left, right)
        made = split(dot_split(split(rest), inverse[j]))
        for i in range(j + 1, blocks):
            rows = slice((i - j - 1) * block, (i - j) * block)
            factor[i, j] = (made[0][rows], made[1][rows])
    new = []
    for j in range(blocks):
        rest = partial_ref[:, j * block : (j + 1) * block]
        if j:
            right = stack([flip(factor[j, k]) for k in range(j)], 0)
            rest = rest - dot_split(stack(new, 1), right)
        result = dot_split(split(rest), inverse[j])
        new.append(split(result))
        half = blocks // 2
        mine = right_side == j // half
        place = pl.ds((j % half) * block, block)

        @pl.when(mine)
        def _():
            keep_ref[:, place] = result

        @pl.when(jnp.logical_not(mine))
        def _():
            give_ref[:, place] = result


def recur(index, partial, mine, other, inv_tiles):
    rows, panel = partial.shape
    blocks = inv_tiles.shape[0]
    rows = rows // SENDS
    half = jax.ShapeDtypeStruct((rows, panel // 2), jnp.float32)
    vmem = pl.BlockSpec(memory_space=pltpu.VMEM)
    return pl.pallas_call(
        functools.partial(recur_kernel, blocks),
        grid=(1,),
        in_specs=[pl.BlockSpec((rows, panel), lambda i: (index, 0)), vmem, vmem, vmem],
        out_specs=[vmem, vmem],
        out_shape=[half, half],
        compiler_params=pltpu.CompilerParams(vmem_limit_bytes=20 << 20),
        name="recur",
    )(*near([partial, mine, other]), inv_tiles)


def finish_kernel(keep_ref, taken_ref, *refs):
    refs[-1][...] = keep_ref[...] + taken_ref[...]


def finish(index, keep, taken, result):
    rows, columns = keep.shape
    vmem = pl.BlockSpec(memory_space=pltpu.VMEM)
    anywhere = pl.BlockSpec(memory_space=pl.ANY)
    old = [] if result is None else [result]
    return pl.pallas_call(
        finish_kernel,
        grid=(1,),
        in_specs=[vmem, vmem] + [anywhere] * len(old),
        out_specs=pl.BlockSpec((rows, columns), lambda i: (index, 0)),
        out_shape=jax.ShapeDtypeStruct((rows * SENDS, columns), jnp.float32),
        input_output_aliases={2: 0} if old else {},
        compiler_params=pltpu.CompilerParams(vmem_limit_bytes=8 << 20),
        name="finish",
    )(*near([keep, taken]), *old)


def lined(*args):
    return lined_panel(*args)


def lined_panel(coeffs, earlier, inv_tiles, piv_local, piv_owner):
    size = lax.axis_size("wide")
    lines = size // GROUP
    me = lax.axis_index("wide")
    panel = piv_local.shape[0]
    blocks = inv_tiles.shape[0]
    capacity = 3 * panel // size
    widths = [source.shape[1] // size for source in (coeffs, earlier)]
    edge = GROUP * widths[0]

    owners = piv_owner[:, 0]
    positions = jnp.arange(panel, dtype=jnp.int32)
    earlier_same = (owners[:, None] == owners[None, :]) & (positions[None, :] < positions[:, None])
    ranks = jnp.sum(earlier_same, axis=1, dtype=jnp.int32)
    hops = tuple(range(lines - 1, -1, -1))
    cuts = (hops,) if ONE_CUT else (hops[: lines // 2], hops[lines // 2 :])
    parts = {}
    for hops in cuts:
        made = cut(hops, lines, capacity, piv_owner, piv_local, coeffs, earlier)
        for index, hop in enumerate(hops):
            for bit in range(GROUP):
                parts[hop * GROUP + bit] = made[index * GROUP + bit]
    got = []
    for bit in range(size):
        got.append(exchange(parts[bit], "wide", bit, size) if bit else parts[bit])
    stacked = jnp.concatenate(got, axis=0)
    places = (owners ^ me) * capacity + ranks
    taken = places[:, None] == jnp.arange(size * capacity, dtype=jnp.int32)[None, :]
    own = lax.dot_general(
        stacked,
        taken.astype(jnp.bfloat16),
        (((0,), (1,)), ((), ())),
        preferred_element_type=jnp.float32,
    ).astype(jnp.bfloat16)

    up, down = own, own
    tables = arrival_order(lines)
    received = {}
    pieces = [own]
    sources = [tuple(range(lines))]
    for hop in range(1, lines):
        rising = [(i, i + GROUP) for i in range(size - GROUP) if i // GROUP >= hop - 1]
        falling = [(i, i - GROUP) for i in range(GROUP, size) if lines - 1 - i // GROUP >= hop - 1]
        down = lax.ppermute(down, "wide", rising)
        up = lax.ppermute(up, "wide", falling)
        received[("down", hop)] = down
        received[("up", hop)] = up
        pieces.append(choose([tables[i][hop - 1][:2] for i in range(lines)], received))
        sources.append(tuple(tables[i][hop - 1][2] for i in range(lines)))

    groups = []
    for piece in pieces:
        across = exchange(piece, "wide", 2, size)
        beside = exchange(piece, "wide", 1, size)
        corner = exchange(across, "wide", 1, size)
        groups.append([piece, beside, across, corner])
    ticks = {hop: tick(owners if hop % 2 else piv_local, hop) for hop in range(1, lines - 1)}
    state = None
    for index, (source, group) in enumerate(zip(sources, groups)):
        final = index == lines - 1
        if final:
            mine = lower_only(blocks, edge, (0, 1), state[1], group[:2])
            mine = lower_only(blocks, edge, (2, 3), mine, group[2:])
        ticked = ticks[min(max(index, 1), lines - 2)]
        state = accumulate(source, blocks, ticked, coeffs, earlier, group, state, final)
    mine = mine + exchange(mine, "narrow", 1, 2)
    other = exchange(mine, "wide", 1, size)
    result = None
    for index in range(SENDS):
        keep, give = recur(index, state[0], mine, other, inv_tiles)
        taken = exchange(give, "narrow", 1, 2)
        result = finish(index, keep, taken, result)
    return result


def on_device(coeffs, earlier, inv_tiles, piv_local, piv_owner):
    chosen = lined if fits(coeffs, earlier, inv_tiles) else general
    return chosen(coeffs, earlier, inv_tiles, piv_local, piv_owner)


def fits(coeffs, earlier, inv_tiles):
    size = lax.axis_size("wide")
    lines = size // GROUP
    return (
        size == lines * GROUP
        and size & (size - 1) == 0
        and lines > 1
        and lax.axis_size("narrow") == 2
        and coeffs.shape[0] % (SUBLANES * TILES) == 0
        and coeffs.shape[1] % (lines * LANES) == 0
        and earlier.shape[1] % (lines * LANES) == 0
        and (coeffs.shape[1] + earlier.shape[1]) % (size * SUBLANES) == 0
        and inv_tiles.shape[0] % 4 == 0
    )


def solution(mesh):
    return jax.shard_map(
        on_device,
        mesh=mesh,
        in_specs=(P("wide", "narrow"), P("wide", "narrow"), P(), P(), P()),
        out_specs=P("wide", "narrow"),
        check_vma=False,
    )
```

```python
import functools

import jax
import jax.numpy as jnp
from jax import lax
from jax.experimental import pallas as pl
from jax.experimental.pallas import tpu as pltpu
from jax.sharding import PartitionSpec as P


LANES = 128
SUBLANES = 16
GROUP = 4
ONE_CUT = True
SENDS = 4
TILES = 2
EXACT = lax.Precision.HIGHEST


def panel_factor(density, diag_block, inv_tiles):
    block_size = inv_tiles.shape[1]
    piv_parts = []
    new_parts = []
    for block_index in range(inv_tiles.shape[0]):
        low_edge = block_index * block_size
        high_edge = low_edge + block_size
        piv_rest = diag_block[:, low_edge:high_edge]
        new_rest = density[:, low_edge:high_edge]
        if block_index > 0:
            piv_left = jnp.concatenate(piv_parts, axis=1)
            new_left = jnp.concatenate(new_parts, axis=1)
            coupling = piv_left[low_edge:high_edge]
            piv_rest = piv_rest - jnp.dot(piv_left, coupling.T, precision=EXACT)
            new_rest = new_rest - jnp.dot(new_left, coupling.T, precision=EXACT)
        piv_parts.append(jnp.dot(piv_rest, inv_tiles[block_index], precision=EXACT))
        new_parts.append(jnp.dot(new_rest, inv_tiles[block_index], precision=EXACT))
    return jnp.concatenate(new_parts, axis=1)


def general(coeffs, earlier, inv_tiles, piv_local, piv_owner):
    owners = piv_owner[:, 0]
    panel_width = piv_local.shape[0]
    mine = owners == lax.axis_index("wide")
    capacity = 3 * panel_width // lax.axis_size("wide")
    positions = jnp.arange(panel_width, dtype=jnp.int32)
    same_owner = owners[:, None] == owners[None, :]
    before = positions[None, :] < positions[:, None]
    slot_rank = jnp.sum(same_owner & before, axis=1)
    slot_index = owners * capacity + slot_rank
    wanted = mine[None, :] & (slot_rank[None, :] == jnp.arange(capacity, dtype=jnp.int32)[:, None])
    local_rows = jnp.sum(jnp.where(wanted, piv_local[None, :], 0), axis=1)
    filled = jnp.any(wanted, axis=1)
    slots = [jnp.where(filled[:, None], source[local_rows], 0) for source in (coeffs, earlier)]
    pieces = [lax.all_gather(slot, "wide", axis=0, tiled=True) for slot in slots]
    select = slot_index[:, None] == jnp.arange(pieces[0].shape[0], dtype=jnp.int32)[None, :]
    select = select.astype(jnp.bfloat16)
    pivots = [
        jnp.dot(select, piece, preferred_element_type=jnp.float32).astype(jnp.bfloat16)
        for piece in pieces
    ]
    partial = [
        jnp.einsum("ro,po->rp", source, pivot, preferred_element_type=jnp.float32)
        for source, pivot in zip((coeffs, earlier), pivots)
    ]
    density = lax.psum_scatter(
        partial[0] - partial[1], "narrow", scatter_dimension=0, tiled=True
    )
    diag = [
        jnp.einsum("qo,po->qp", pivot, pivot, preferred_element_type=jnp.float32)
        for pivot in pivots
    ]
    diag_block = lax.psum(diag[0] - diag[1], "narrow")
    factor = panel_factor(density, diag_block, inv_tiles)
    return lax.all_to_all(factor, "narrow", split_axis=1, concat_axis=0, tiled=True)


def look_up(table, line):
    result = jnp.int32(table[-1])
    for index, entry in enumerate(table[:-1]):
        result = jnp.where(line == index, jnp.int32(entry), result)
    return result


def exchange(value, axis, bit, size):
    return lax.ppermute(value, axis, [(i, i ^ bit) for i in range(size)])


def lower_pairs(blocks):
    pairs = [(i, j) for i in range(blocks) for j in range(i)]
    half = len(pairs) // 2
    return pairs[:half], pairs[half:]


def near(values):
    return [pltpu.with_memory_space_constraint(value, pltpu.VMEM) for value in values]


def away(values):
    return [pltpu.with_memory_space_constraint(value, pltpu.HBM) for value in values]


def seat():
    me = lax.axis_index("wide")
    return lax.div(me, GROUP), lax.rem(me, GROUP)


def hold_copies(lane, pieces, held_ref, sems):
    width = pieces[0].shape[0]
    copies = []
    for index, piece in enumerate(pieces):
        start = pl.multiple_of((lane ^ index) * width, SUBLANES)
        target = held_ref.at[pl.ds(start, width), :]
        copies.append(pltpu.make_async_copy(piece, target, sems.at[index]))
    return copies


def add_lower(blocks, edge, lane, held_ref, old_ref, lower_ref):
    block = held_ref.shape[1] // blocks
    for parity, pairs in enumerate(lower_pairs(blocks)):

        @pl.when((lane & 1) == parity)
        def _():
            place = 0
            for i in sorted({pair[0] for pair in pairs}):
                picks = [pair[1] for pair in pairs if pair[0] == i]
                rows = slice(i * block, (i + 1) * block)
                columns = slice(picks[0] * block, (picks[-1] + 1) * block)
                terms = [
                    lax.dot_general(
                        held_ref[part, rows],
                        held_ref[part, columns],
                        (((0,), (0,)), ((), ())),
                        preferred_element_type=jnp.float32,
                    )
                    for part in (slice(0, edge), slice(edge, held_ref.shape[0]))
                ]
                total = terms[0] - terms[1]
                for index in range(len(picks)):
                    part = total[:, index * block : (index + 1) * block]
                    if old_ref is not None:
                        part = old_ref[place] + part
                    lower_ref[place] = part
                    place += 1


def lower_kernel(blocks, edge, bits, old_ref, *refs):
    pieces, lower_ref = refs[:-1], refs[-1]
    _, lane = seat()
    width, panel = pieces[0].shape
    block = panel // blocks
    signed = []
    for bit, piece in zip(bits, pieces):
        at = (lane ^ bit) * width + lax.broadcasted_iota(jnp.int32, (width, block), 0)
        signed.append(jnp.where(at < edge, 1.0, -1.0).astype(jnp.bfloat16))
    for parity, pairs in enumerate(lower_pairs(blocks)):

        @pl.when((lane & 1) == parity)
        def _():
            place = 0
            for i in sorted({pair[0] for pair in pairs}):
                picks = [pair[1] for pair in pairs if pair[0] == i]
                columns = slice(picks[0] * block, (picks[-1] + 1) * block)
                total = 0.0
                for sign, piece in zip(signed, pieces):
                    total = total + lax.dot_general(
                        piece[:, i * block : (i + 1) * block] * sign,
                        piece[:, columns],
                        (((0,), (0,)), ((), ())),
                        preferred_element_type=jnp.float32,
                    )
                for index in range(len(picks)):
                    part = total[:, index * block : (index + 1) * block]
                    lower_ref[place] = old_ref[place] + part
                    place += 1


def lower_only(blocks, edge, bits, old, pieces):
    vmem = pl.BlockSpec(memory_space=pltpu.VMEM)
    return pl.pallas_call(
        functools.partial(lower_kernel, blocks, edge, bits),
        in_specs=[vmem] * (1 + len(pieces)),
        out_specs=vmem,
        out_shape=jax.ShapeDtypeStruct(old.shape, jnp.float32),
        input_output_aliases={0: 0},
        compiler_params=pltpu.CompilerParams(vmem_limit_bytes=8 << 20),
        name="lower",
    )(*near([old, *pieces]))


def accumulate_kernel(table, blocks, fresh, final, tick_ref, coeffs_ref, earlier_ref, *refs):
    pieces, refs = list(refs[:GROUP]), list(refs[GROUP:])
    old_sum_ref = None if fresh else refs.pop(0)
    old_lower_ref = None if fresh or final else refs.pop(0)
    sum_ref = refs.pop(0)
    lower_ref = None if final else refs.pop(0)
    held_ref, main_ref, sems = refs
    line, lane = seat()
    source = look_up(table, line)
    tile = main_ref.shape[0] // TILES
    depths = [ref.shape[1] // len(table) for ref in (coeffs_ref, earlier_ref)]
    holds = hold_copies(lane, pieces, held_ref, sems)
    loads = []
    for step in range(TILES):
        rows_at = pl.ds(step * tile, tile)
        place = 0
        for side, (ref, depth) in enumerate(zip((coeffs_ref, earlier_ref), depths)):
            base = pl.multiple_of(source * depth, LANES)
            loads.append(
                pltpu.make_async_copy(
                    ref.at[rows_at, pl.ds(base, depth)],
                    main_ref.at[rows_at, pl.ds(place, depth)],
                    sems.at[GROUP + 2 * step + side],
                )
            )
            place += depth
    for copy in holds + loads:
        copy.start()
    for copy in holds:
        copy.wait()
    if not final:
        add_lower(blocks, depths[0], lane, held_ref, old_lower_ref, lower_ref)
    for step in range(TILES):
        loads[2 * step].wait()
        loads[2 * step + 1].wait()
        rows_at = slice(step * tile, (step + 1) * tile)
        total = jnp.dot(main_ref[rows_at, :], held_ref[...], preferred_element_type=jnp.float32)
        sum_ref[rows_at, :] = total if fresh else old_sum_ref[rows_at, :] + total


def accumulate(table, blocks, ticked, coeffs, earlier, pieces, state, final):
    rows = coeffs.shape[0]
    width, panel = pieces[0].shape
    fresh = state is None
    block = panel // blocks
    shapes = [(rows, panel), (len(lower_pairs(blocks)[0]), block, block)]
    state = [] if fresh else list(state)
    if final:
        shapes, state = shapes[:1], state[:1]
    anywhere = pl.BlockSpec(memory_space=pl.ANY)
    vmem = pl.BlockSpec(memory_space=pltpu.VMEM)
    return pl.pallas_call(
        functools.partial(accumulate_kernel, table, blocks, fresh, final),
        in_specs=[anywhere] * 3
        + [vmem] * (GROUP + len(state)),
        out_specs=[vmem] * len(shapes),
        scratch_shapes=[
            pltpu.VMEM((width * GROUP, panel), jnp.bfloat16),
            pltpu.VMEM((rows, width * GROUP), jnp.bfloat16),
            pltpu.SemaphoreType.DMA((GROUP + 2 * TILES,)),
        ],
        out_shape=[jax.ShapeDtypeStruct(shape, jnp.float32) for shape in shapes],
        input_output_aliases={3 + GROUP + i: i for i in range(len(state))},
        cost_estimate=pl.CostEstimate(
            flops=2 * rows * panel * width * GROUP,
            bytes_accessed=2 * rows * width * GROUP,
            transcendentals=0,
        ),
        compiler_params=pltpu.CompilerParams(vmem_limit_bytes=16 << 20),
        name="accumulate",
    )(ticked, *away([coeffs, earlier]), *near([*pieces, *state]))


def my_rows(capacity, pivot_ref):
    panel = pivot_ref.shape[1]
    below = lax.broadcasted_iota(jnp.int32, (panel, panel), 0)
    across = lax.broadcasted_iota(jnp.int32, (panel, panel), 1)
    turned = pivot_ref[0:1, :]
    owners = jnp.sum(jnp.where(below == across, turned, 0), axis=1, keepdims=True)
    same = (owners == turned) & (below < across)
    ranks = jnp.sum(jnp.where(same, 1, 0), axis=0, keepdims=True)
    slots = lax.broadcasted_iota(jnp.int32, (capacity, panel), 0)
    wanted = (ranks == slots) & (turned == lax.axis_index("wide"))
    return jnp.sum(jnp.where(wanted, pivot_ref[1:2, :] + 1, 0), axis=1, keepdims=True) - 1


def cut_kernel(hops, lines, pivot_ref, coeffs_ref, earlier_ref, *refs):
    outs, (main_ref, sems) = refs[:-2], refs[-2:]
    line, lane = seat()
    depths = [ref.shape[1] // lines for ref in (coeffs_ref, earlier_ref)]
    width = sum(depths) // GROUP
    copies = []
    for index, hop in enumerate(hops):
        place = 0
        for side, (ref, depth) in enumerate(zip((coeffs_ref, earlier_ref), depths)):
            base = pl.multiple_of((line ^ hop) * depth, LANES)
            source = ref.at[:, pl.ds(base, depth)]
            target = main_ref.at[index, :, pl.ds(place, depth)]
            copies.append(pltpu.make_async_copy(source, target, sems.at[index, side]))
            place += depth
    for copy in copies:
        copy.start()
    capacity = outs[0].shape[0]
    at = lax.broadcasted_iota(jnp.int32, (capacity, coeffs_ref.shape[0]), 1)
    select = my_rows(capacity, pivot_ref) == at
    select = jnp.where(select, 1.0, 0.0).astype(jnp.bfloat16)
    for index in range(len(hops)):
        copies[2 * index].wait()
        copies[2 * index + 1].wait()
        rows = jnp.dot(select, main_ref[index], preferred_element_type=jnp.float32)
        rows = jnp.concatenate([rows[:, : depths[0]], -rows[:, depths[0] :]], axis=1)
        rows = rows.astype(jnp.bfloat16)
        parts = [rows[:, i * width : (i + 1) * width] for i in range(GROUP)]
        for case in range(GROUP):

            @pl.when(lane == case)
            def _():
                for i, part in enumerate(parts):
                    outs[index * GROUP + (i ^ case)][...] = part


def cut(hops, lines, capacity, piv_owner, piv_local, coeffs, earlier):
    vmem = pl.BlockSpec(memory_space=pltpu.VMEM)
    anywhere = pl.BlockSpec(memory_space=pl.ANY)
    total = coeffs.shape[1] + earlier.shape[1]
    pivots = jnp.concatenate([piv_owner.reshape(1, -1), piv_local[None, :]], axis=0)
    pivots = near([pivots])[0]
    shape = jax.ShapeDtypeStruct((capacity, total // (lines * GROUP)), jnp.bfloat16)
    return pl.pallas_call(
        functools.partial(cut_kernel, hops, lines),
        in_specs=[vmem, anywhere, anywhere],
        out_specs=[vmem] * (len(hops) * GROUP),
        out_shape=[shape] * (len(hops) * GROUP),
        scratch_shapes=[
            pltpu.VMEM((len(hops), coeffs.shape[0], total // lines), jnp.bfloat16),
            pltpu.SemaphoreType.DMA((len(hops), 2)),
        ],
        compiler_params=pltpu.CompilerParams(vmem_limit_bytes=24 << 20),
        name="cut",
    )(pivots, *away([coeffs, earlier]))


def tick(local, hop):
    return local * (hop + 2) + hop


def choose_kernel(order, *refs):
    which = look_up(order, seat()[0])
    for index, source in enumerate(refs[:-1]):

        @pl.when(which == index)
        def _():
            refs[-1][...] = source[...]


def choose(table, received):
    names = sorted(set(table))
    vmem = pl.BlockSpec(memory_space=pltpu.VMEM)
    sources = [received[name] for name in names]
    return pl.pallas_call(
        functools.partial(choose_kernel, tuple(names.index(name) for name in table)),
        in_specs=[vmem] * len(names),
        out_specs=vmem,
        out_shape=jax.ShapeDtypeStruct(sources[0].shape, sources[0].dtype),
        compiler_params=pltpu.CompilerParams(vmem_limit_bytes=4 << 20),
        name="choose",
    )(*near(sources))


def split(value):
    high = value.astype(jnp.bfloat16)
    return high, (value - high.astype(jnp.float32)).astype(jnp.bfloat16)


def dot_split(left, right):
    left = jnp.concatenate([left[0], left[0], left[1]], axis=1)
    right = jnp.concatenate([right[0], right[1], right[0]], axis=0)
    return jnp.dot(left, right, preferred_element_type=jnp.float32)


def recur_kernel(blocks, partial_ref, mine_ref, other_ref, inv_ref, keep_ref, give_ref):
    block = inv_ref.shape[1]
    odd = (seat()[1] & 1) == 1
    right_side = lax.axis_index("narrow")
    lower = {}
    for parity, pairs in enumerate(lower_pairs(blocks)):
        here = odd if parity else jnp.logical_not(odd)
        for index, pair in enumerate(pairs):
            lower[pair] = jnp.where(here, mine_ref[index], other_ref[index])
    inverse = [split(inv_ref[j]) for j in range(blocks)]

    def stack(parts, axis):
        return tuple(jnp.concatenate(side, axis=axis) for side in zip(*parts))

    def flip(part):
        return tuple(jnp.transpose(side) for side in part)

    factor = {}
    for j in range(blocks - 1):
        rest = jnp.concatenate(
            [lower[i, j] for i in range(j + 1, blocks)], axis=0
        )
        if j:
            left = stack([stack([factor[i, k] for k in range(j)], 1) for i in range(j + 1, blocks)], 0)
            right = stack([flip(factor[j, k]) for k in range(j)], 0)
            rest = rest - dot_split(left, right)
        made = split(dot_split(split(rest), inverse[j]))
        for i in range(j + 1, blocks):
            rows = slice((i - j - 1) * block, (i - j) * block)
            factor[i, j] = (made[0][rows], made[1][rows])
    new = []
    for j in range(blocks):
        rest = partial_ref[:, j * block : (j + 1) * block]
        if j:
            right = stack([flip(factor[j, k]) for k in range(j)], 0)
            rest = rest - dot_split(stack(new, 1), right)
        result = dot_split(split(rest), inverse[j])
        new.append(split(result))
        half = blocks // 2
        mine = right_side == j // half
        place = pl.ds((j % half) * block, block)

        @pl.when(mine)
        def _():
            keep_ref[:, place] = result

        @pl.when(jnp.logical_not(mine))
        def _():
            give_ref[:, place] = result


def recur(index, partial, mine, other, inv_tiles):
    rows, panel = partial.shape
    blocks = inv_tiles.shape[0]
    rows = rows // SENDS
    half = jax.ShapeDtypeStruct((rows, panel // 2), jnp.float32)
    vmem = pl.BlockSpec(memory_space=pltpu.VMEM)
    return pl.pallas_call(
        functools.partial(recur_kernel, blocks),
        grid=(1,),
        in_specs=[pl.BlockSpec((rows, panel), lambda i: (index, 0)), vmem, vmem, vmem],
        out_specs=[vmem, vmem],
        out_shape=[half, half],
        compiler_params=pltpu.CompilerParams(vmem_limit_bytes=20 << 20),
        name="recur",
    )(*near([partial, mine, other]), inv_tiles)


def finish_kernel(keep_ref, taken_ref, *refs):
    refs[-1][...] = keep_ref[...] + taken_ref[...]


def finish(index, keep, taken, result):
    rows, columns = keep.shape
    vmem = pl.BlockSpec(memory_space=pltpu.VMEM)
    anywhere = pl.BlockSpec(memory_space=pl.ANY)
    old = [] if result is None else [result]
    return pl.pallas_call(
        finish_kernel,
        grid=(1,),
        in_specs=[vmem, vmem] + [anywhere] * len(old),
        out_specs=pl.BlockSpec((rows, columns), lambda i: (index, 0)),
        out_shape=jax.ShapeDtypeStruct((rows * SENDS, columns), jnp.float32),
        input_output_aliases={2: 0} if old else {},
        compiler_params=pltpu.CompilerParams(vmem_limit_bytes=8 << 20),
        name="finish",
    )(*near([keep, taken]), *old)


def lined(*args):
    return lined_panel(*args)


def lined_panel(coeffs, earlier, inv_tiles, piv_local, piv_owner):
    size = lax.axis_size("wide")
    lines = size // GROUP
    me = lax.axis_index("wide")
    panel = piv_local.shape[0]
    blocks = inv_tiles.shape[0]
    capacity = 3 * panel // size
    widths = [source.shape[1] // size for source in (coeffs, earlier)]
    edge = GROUP * widths[0]

    owners = piv_owner[:, 0]
    positions = jnp.arange(panel, dtype=jnp.int32)
    earlier_same = (owners[:, None] == owners[None, :]) & (positions[None, :] < positions[:, None])
    ranks = jnp.sum(earlier_same, axis=1, dtype=jnp.int32)
    hops = tuple(range(lines - 1, -1, -1))
    cuts = (hops,) if ONE_CUT else (hops[: lines // 2], hops[lines // 2 :])
    parts = {}
    for hops in cuts:
        made = cut(hops, lines, capacity, piv_owner, piv_local, coeffs, earlier)
        for index, hop in enumerate(hops):
            for bit in range(GROUP):
                parts[hop * GROUP + bit] = made[index * GROUP + bit]
    got = []
    for bit in range(size):
        got.append(exchange(parts[bit], "wide", bit, size) if bit else parts[bit])
    stacked = jnp.concatenate(got, axis=0)
    places = (owners ^ me) * capacity + ranks
    taken = places[:, None] == jnp.arange(size * capacity, dtype=jnp.int32)[None, :]
    own = lax.dot_general(
        stacked,
        taken.astype(jnp.bfloat16),
        (((0,), (1,)), ((), ())),
        preferred_element_type=jnp.float32,
    ).astype(jnp.bfloat16)

    def swap_middle(value):
        pairs = [(i, i ^ (3 * GROUP)) for i in range(size) if i // GROUP in (1, 2)]
        return lax.ppermute(value, "wide", pairs)

    def send_out(value):
        pairs = [(i, i ^ GROUP) for i in range(size) if i // GROUP in (1, 2)]
        return lax.ppermute(value, "wide", pairs)

    pair = exchange(own, "wide", GROUP, size)
    middle = swap_middle(own)
    farther = swap_middle(pair)
    out = send_out(middle)
    last_out = send_out(farther)
    table = ["out", "middle", "middle", "out"]
    third = choose(table, {"out": out, "middle": middle})
    fourth = choose(table, {"out": last_out, "middle": farther})
    pieces = [own, pair, third, fourth]
    sources = [(0, 1, 2, 3), (1, 0, 3, 2), (2, 2, 1, 1), (3, 3, 0, 0)]

    groups = []
    for piece in pieces:
        across = exchange(piece, "wide", 2, size)
        beside = exchange(piece, "wide", 1, size)
        corner = exchange(across, "wide", 1, size)
        groups.append([piece, beside, across, corner])
    ticks = {hop: tick(owners if hop % 2 else piv_local, hop) for hop in range(1, lines - 1)}
    state = None
    for index, (source, group) in enumerate(zip(sources, groups)):
        final = index == lines - 1
        if final:
            mine = lower_only(blocks, edge, (0, 1), state[1], group[:2])
            mine = lower_only(blocks, edge, (2, 3), mine, group[2:])
        ticked = ticks[min(max(index, 1), lines - 2)]
        state = accumulate(source, blocks, ticked, coeffs, earlier, group, state, final)
    mine = mine + exchange(mine, "narrow", 1, 2)
    other = exchange(mine, "wide", 1, size)
    result = None
    for index in range(SENDS):
        keep, give = recur(index, state[0], mine, other, inv_tiles)
        taken = exchange(give, "narrow", 1, 2)
        result = finish(index, keep, taken, result)
    return result


def on_device(coeffs, earlier, inv_tiles, piv_local, piv_owner):
    chosen = lined if fits(coeffs, earlier, inv_tiles) else general
    return chosen(coeffs, earlier, inv_tiles, piv_local, piv_owner)


def fits(coeffs, earlier, inv_tiles):
    size = lax.axis_size("wide")
    lines = size // GROUP
    return (
        size == lines * GROUP
        and size & (size - 1) == 0
        and lines == 4
        and lax.axis_size("narrow") == 2
        and coeffs.shape[0] % (SUBLANES * TILES) == 0
        and coeffs.shape[1] % (lines * LANES) == 0
        and earlier.shape[1] % (lines * LANES) == 0
        and (coeffs.shape[1] + earlier.shape[1]) % (size * SUBLANES) == 0
        and inv_tiles.shape[0] % 4 == 0
    )


def solution(mesh):
    return jax.shard_map(
        on_device,
        mesh=mesh,
        in_specs=(P("wide", "narrow"), P("wide", "narrow"), P(), P(), P()),
        out_specs=P("wide", "narrow"),
        check_vma=False,
    )
```

```python
import functools

import jax
import jax.numpy as jnp
from jax import lax
from jax.experimental import pallas as pl
from jax.experimental.pallas import tpu as pltpu
from jax.sharding import PartitionSpec as P


LANES = 128
SUBLANES = 16
GROUP = 4
ONE_CUT = True
SENDS = 4
TILES = 2
EXACT = lax.Precision.HIGHEST


def panel_factor(density, diag_block, inv_tiles):
    block_size = inv_tiles.shape[1]
    piv_parts = []
    new_parts = []
    for block_index in range(inv_tiles.shape[0]):
        low_edge = block_index * block_size
        high_edge = low_edge + block_size
        piv_rest = diag_block[:, low_edge:high_edge]
        new_rest = density[:, low_edge:high_edge]
        if block_index > 0:
            piv_left = jnp.concatenate(piv_parts, axis=1)
            new_left = jnp.concatenate(new_parts, axis=1)
            coupling = piv_left[low_edge:high_edge]
            piv_rest = piv_rest - jnp.dot(piv_left, coupling.T, precision=EXACT)
            new_rest = new_rest - jnp.dot(new_left, coupling.T, precision=EXACT)
        piv_parts.append(jnp.dot(piv_rest, inv_tiles[block_index], precision=EXACT))
        new_parts.append(jnp.dot(new_rest, inv_tiles[block_index], precision=EXACT))
    return jnp.concatenate(new_parts, axis=1)


def general(coeffs, earlier, inv_tiles, piv_local, piv_owner):
    owners = piv_owner[:, 0]
    panel_width = piv_local.shape[0]
    mine = owners == lax.axis_index("wide")
    capacity = 3 * panel_width // lax.axis_size("wide")
    positions = jnp.arange(panel_width, dtype=jnp.int32)
    same_owner = owners[:, None] == owners[None, :]
    before = positions[None, :] < positions[:, None]
    slot_rank = jnp.sum(same_owner & before, axis=1)
    slot_index = owners * capacity + slot_rank
    wanted = mine[None, :] & (slot_rank[None, :] == jnp.arange(capacity, dtype=jnp.int32)[:, None])
    local_rows = jnp.sum(jnp.where(wanted, piv_local[None, :], 0), axis=1)
    filled = jnp.any(wanted, axis=1)
    slots = [jnp.where(filled[:, None], source[local_rows], 0) for source in (coeffs, earlier)]
    pieces = [lax.all_gather(slot, "wide", axis=0, tiled=True) for slot in slots]
    select = slot_index[:, None] == jnp.arange(pieces[0].shape[0], dtype=jnp.int32)[None, :]
    select = select.astype(jnp.bfloat16)
    pivots = [
        jnp.dot(select, piece, preferred_element_type=jnp.float32).astype(jnp.bfloat16)
        for piece in pieces
    ]
    partial = [
        jnp.einsum("ro,po->rp", source, pivot, preferred_element_type=jnp.float32)
        for source, pivot in zip((coeffs, earlier), pivots)
    ]
    density = lax.psum_scatter(
        partial[0] - partial[1], "narrow", scatter_dimension=0, tiled=True
    )
    diag = [
        jnp.einsum("qo,po->qp", pivot, pivot, preferred_element_type=jnp.float32)
        for pivot in pivots
    ]
    diag_block = lax.psum(diag[0] - diag[1], "narrow")
    factor = panel_factor(density, diag_block, inv_tiles)
    return lax.all_to_all(factor, "narrow", split_axis=1, concat_axis=0, tiled=True)


def look_up(table, line):
    result = jnp.int32(table[-1])
    for index, entry in enumerate(table[:-1]):
        result = jnp.where(line == index, jnp.int32(entry), result)
    return result


def exchange(value, axis, bit, size):
    return lax.ppermute(value, axis, [(i, i ^ bit) for i in range(size)])


def lower_pairs(blocks):
    pairs = [(i, j) for i in range(blocks) for j in range(i)]
    half = len(pairs) // 2
    return pairs[:half], pairs[half:]


def near(values):
    return [pltpu.with_memory_space_constraint(value, pltpu.VMEM) for value in values]


def away(values):
    return [pltpu.with_memory_space_constraint(value, pltpu.HBM) for value in values]


def seat():
    me = lax.axis_index("wide")
    return lax.div(me, GROUP), lax.rem(me, GROUP)


def hold_copies(lane, pieces, held_ref, sems):
    width = pieces[0].shape[0]
    copies = []
    for index, piece in enumerate(pieces):
        start = pl.multiple_of((lane ^ index) * width, SUBLANES)
        target = held_ref.at[pl.ds(start, width), :]
        copies.append(pltpu.make_async_copy(piece, target, sems.at[index]))
    return copies


def add_lower(blocks, edge, lane, held_ref, old_ref, lower_ref):
    block = held_ref.shape[1] // blocks
    for parity, pairs in enumerate(lower_pairs(blocks)):

        @pl.when((lane & 1) == parity)
        def _():
            place = 0
            for i in sorted({pair[0] for pair in pairs}):
                picks = [pair[1] for pair in pairs if pair[0] == i]
                rows = slice(i * block, (i + 1) * block)
                columns = slice(picks[0] * block, (picks[-1] + 1) * block)
                terms = [
                    lax.dot_general(
                        held_ref[part, rows],
                        held_ref[part, columns],
                        (((0,), (0,)), ((), ())),
                        preferred_element_type=jnp.float32,
                    )
                    for part in (slice(0, edge), slice(edge, held_ref.shape[0]))
                ]
                total = terms[0] - terms[1]
                for index in range(len(picks)):
                    part = total[:, index * block : (index + 1) * block]
                    if old_ref is not None:
                        part = old_ref[place] + part
                    lower_ref[place] = part
                    place += 1


def lower_kernel(blocks, edge, bits, old_ref, *refs):
    pieces, lower_ref = refs[:-1], refs[-1]
    _, lane = seat()
    width, panel = pieces[0].shape
    block = panel // blocks
    signed = []
    for bit, piece in zip(bits, pieces):
        at = (lane ^ bit) * width + lax.broadcasted_iota(jnp.int32, (width, block), 0)
        signed.append(jnp.where(at < edge, 1.0, -1.0).astype(jnp.bfloat16))
    for parity, pairs in enumerate(lower_pairs(blocks)):

        @pl.when((lane & 1) == parity)
        def _():
            place = 0
            for i in sorted({pair[0] for pair in pairs}):
                picks = [pair[1] for pair in pairs if pair[0] == i]
                columns = slice(picks[0] * block, (picks[-1] + 1) * block)
                total = 0.0
                for sign, piece in zip(signed, pieces):
                    total = total + lax.dot_general(
                        piece[:, i * block : (i + 1) * block] * sign,
                        piece[:, columns],
                        (((0,), (0,)), ((), ())),
                        preferred_element_type=jnp.float32,
                    )
                for index in range(len(picks)):
                    part = total[:, index * block : (index + 1) * block]
                    lower_ref[place] = old_ref[place] + part
                    place += 1


def lower_only(blocks, edge, bits, old, pieces):
    vmem = pl.BlockSpec(memory_space=pltpu.VMEM)
    return pl.pallas_call(
        functools.partial(lower_kernel, blocks, edge, bits),
        in_specs=[vmem] * (1 + len(pieces)),
        out_specs=vmem,
        out_shape=jax.ShapeDtypeStruct(old.shape, jnp.float32),
        input_output_aliases={0: 0},
        compiler_params=pltpu.CompilerParams(vmem_limit_bytes=8 << 20),
        name="lower",
    )(*near([old, *pieces]))


def accumulate_kernel(table, blocks, fresh, final, tick_ref, coeffs_ref, earlier_ref, *refs):
    pieces, refs = list(refs[:GROUP]), list(refs[GROUP:])
    old_sum_ref = None if fresh else refs.pop(0)
    old_lower_ref = None if fresh or final else refs.pop(0)
    sum_ref = refs.pop(0)
    lower_ref = None if final else refs.pop(0)
    held_ref, main_ref, sems = refs
    line, lane = seat()
    source = look_up(table, line)
    tile = main_ref.shape[0] // TILES
    depths = [ref.shape[1] // len(table) for ref in (coeffs_ref, earlier_ref)]
    holds = hold_copies(lane, pieces, held_ref, sems)
    loads = []
    for step in range(TILES):
        rows_at = pl.ds(step * tile, tile)
        place = 0
        for side, (ref, depth) in enumerate(zip((coeffs_ref, earlier_ref), depths)):
            base = pl.multiple_of(source * depth, LANES)
            loads.append(
                pltpu.make_async_copy(
                    ref.at[rows_at, pl.ds(base, depth)],
                    main_ref.at[rows_at, pl.ds(place, depth)],
                    sems.at[GROUP + 2 * step + side],
                )
            )
            place += depth
    for copy in holds + loads:
        copy.start()
    for copy in holds:
        copy.wait()
    if not final:
        add_lower(blocks, depths[0], lane, held_ref, old_lower_ref, lower_ref)
    for step in range(TILES):
        loads[2 * step].wait()
        loads[2 * step + 1].wait()
        rows_at = slice(step * tile, (step + 1) * tile)
        total = jnp.dot(main_ref[rows_at, :], held_ref[...], preferred_element_type=jnp.float32)
        sum_ref[rows_at, :] = total if fresh else old_sum_ref[rows_at, :] + total


def accumulate(table, blocks, ticked, coeffs, earlier, pieces, state, final):
    rows = coeffs.shape[0]
    width, panel = pieces[0].shape
    fresh = state is None
    block = panel // blocks
    shapes = [(rows, panel), (len(lower_pairs(blocks)[0]), block, block)]
    state = [] if fresh else list(state)
    if final:
        shapes, state = shapes[:1], state[:1]
    anywhere = pl.BlockSpec(memory_space=pl.ANY)
    vmem = pl.BlockSpec(memory_space=pltpu.VMEM)
    return pl.pallas_call(
        functools.partial(accumulate_kernel, table, blocks, fresh, final),
        in_specs=[anywhere] * 3
        + [vmem] * (GROUP + len(state)),
        out_specs=[vmem] * len(shapes),
        scratch_shapes=[
            pltpu.VMEM((width * GROUP, panel), jnp.bfloat16),
            pltpu.VMEM((rows, width * GROUP), jnp.bfloat16),
            pltpu.SemaphoreType.DMA((GROUP + 2 * TILES,)),
        ],
        out_shape=[jax.ShapeDtypeStruct(shape, jnp.float32) for shape in shapes],
        input_output_aliases={3 + GROUP + i: i for i in range(len(state))},
        cost_estimate=pl.CostEstimate(
            flops=2 * rows * panel * width * GROUP,
            bytes_accessed=2 * rows * width * GROUP,
            transcendentals=0,
        ),
        compiler_params=pltpu.CompilerParams(vmem_limit_bytes=16 << 20),
        name="accumulate",
    )(ticked, *away([coeffs, earlier]), *near([*pieces, *state]))


def my_rows(capacity, pivot_ref):
    panel = pivot_ref.shape[1]
    below = lax.broadcasted_iota(jnp.int32, (panel, panel), 0)
    across = lax.broadcasted_iota(jnp.int32, (panel, panel), 1)
    turned = pivot_ref[0:1, :]
    owners = jnp.sum(jnp.where(below == across, turned, 0), axis=1, keepdims=True)
    same = (owners == turned) & (below < across)
    ranks = jnp.sum(jnp.where(same, 1, 0), axis=0, keepdims=True)
    slots = lax.broadcasted_iota(jnp.int32, (capacity, panel), 0)
    wanted = (ranks == slots) & (turned == lax.axis_index("wide"))
    return jnp.sum(jnp.where(wanted, pivot_ref[1:2, :] + 1, 0), axis=1, keepdims=True) - 1


def cut_kernel(hops, lines, pivot_ref, coeffs_ref, earlier_ref, *refs):
    outs, (main_ref, sems) = refs[:-2], refs[-2:]
    line, lane = seat()
    depths = [ref.shape[1] // lines for ref in (coeffs_ref, earlier_ref)]
    width = sum(depths) // GROUP
    copies = []
    for index, hop in enumerate(hops):
        place = 0
        for side, (ref, depth) in enumerate(zip((coeffs_ref, earlier_ref), depths)):
            base = pl.multiple_of((line ^ hop) * depth, LANES)
            source = ref.at[:, pl.ds(base, depth)]
            target = main_ref.at[index, :, pl.ds(place, depth)]
            copies.append(pltpu.make_async_copy(source, target, sems.at[index, side]))
            place += depth
    for copy in copies:
        copy.start()
    capacity = outs[0].shape[0]
    at = lax.broadcasted_iota(jnp.int32, (capacity, coeffs_ref.shape[0]), 1)
    select = my_rows(capacity, pivot_ref) == at
    select = jnp.where(select, 1.0, 0.0).astype(jnp.bfloat16)
    for index in range(len(hops)):
        copies[2 * index].wait()
        copies[2 * index + 1].wait()
        rows = jnp.dot(select, main_ref[index], preferred_element_type=jnp.float32)
        rows = jnp.concatenate([rows[:, : depths[0]], -rows[:, depths[0] :]], axis=1)
        rows = rows.astype(jnp.bfloat16)
        parts = [rows[:, i * width : (i + 1) * width] for i in range(GROUP)]
        for case in range(GROUP):

            @pl.when(lane == case)
            def _():
                for i, part in enumerate(parts):
                    outs[index * GROUP + (i ^ case)][...] = part


def cut(hops, lines, capacity, piv_owner, piv_local, coeffs, earlier):
    vmem = pl.BlockSpec(memory_space=pltpu.VMEM)
    anywhere = pl.BlockSpec(memory_space=pl.ANY)
    total = coeffs.shape[1] + earlier.shape[1]
    pivots = jnp.concatenate([piv_owner.reshape(1, -1), piv_local[None, :]], axis=0)
    pivots = near([pivots])[0]
    shape = jax.ShapeDtypeStruct((capacity, total // (lines * GROUP)), jnp.bfloat16)
    return pl.pallas_call(
        functools.partial(cut_kernel, hops, lines),
        in_specs=[vmem, anywhere, anywhere],
        out_specs=[vmem] * (len(hops) * GROUP),
        out_shape=[shape] * (len(hops) * GROUP),
        scratch_shapes=[
            pltpu.VMEM((len(hops), coeffs.shape[0], total // lines), jnp.bfloat16),
            pltpu.SemaphoreType.DMA((len(hops), 2)),
        ],
        compiler_params=pltpu.CompilerParams(vmem_limit_bytes=24 << 20),
        name="cut",
    )(pivots, *away([coeffs, earlier]))


def tick(local, hop):
    return local * (hop + 2) + hop


def choose_kernel(order, *refs):
    which = look_up(order, seat()[0])
    for index, source in enumerate(refs[:-1]):

        @pl.when(which == index)
        def _():
            refs[-1][...] = source[...]


def choose(table, received):
    names = sorted(set(table))
    vmem = pl.BlockSpec(memory_space=pltpu.VMEM)
    sources = [received[name] for name in names]
    return pl.pallas_call(
        functools.partial(choose_kernel, tuple(names.index(name) for name in table)),
        in_specs=[vmem] * len(names),
        out_specs=vmem,
        out_shape=jax.ShapeDtypeStruct(sources[0].shape, sources[0].dtype),
        compiler_params=pltpu.CompilerParams(vmem_limit_bytes=4 << 20),
        name="choose",
    )(*near(sources))


def split(value):
    high = value.astype(jnp.bfloat16)
    return high, (value - high.astype(jnp.float32)).astype(jnp.bfloat16)


def dot_split(left, right):
    left = jnp.concatenate([left[0], left[0], left[1]], axis=1)
    right = jnp.concatenate([right[0], right[1], right[0]], axis=0)
    return jnp.dot(left, right, preferred_element_type=jnp.float32)


def recur_kernel(blocks, partial_ref, mine_ref, other_ref, inv_ref, keep_ref, give_ref):
    block = inv_ref.shape[1]
    odd = (seat()[1] & 1) == 1
    right_side = lax.axis_index("narrow")
    lower = {}
    for parity, pairs in enumerate(lower_pairs(blocks)):
        here = odd if parity else jnp.logical_not(odd)
        for index, pair in enumerate(pairs):
            lower[pair] = jnp.where(here, mine_ref[index], other_ref[index])
    inverse = [split(inv_ref[j]) for j in range(blocks)]

    def stack(parts, axis):
        return tuple(jnp.concatenate(side, axis=axis) for side in zip(*parts))

    def flip(part):
        return tuple(jnp.transpose(side) for side in part)

    factor = {}
    for j in range(blocks - 1):
        rest = jnp.concatenate(
            [lower[i, j] for i in range(j + 1, blocks)], axis=0
        )
        if j:
            left = stack([stack([factor[i, k] for k in range(j)], 1) for i in range(j + 1, blocks)], 0)
            right = stack([flip(factor[j, k]) for k in range(j)], 0)
            rest = rest - dot_split(left, right)
        made = split(dot_split(split(rest), inverse[j]))
        for i in range(j + 1, blocks):
            rows = slice((i - j - 1) * block, (i - j) * block)
            factor[i, j] = (made[0][rows], made[1][rows])
    new = []
    for j in range(blocks):
        rest = partial_ref[:, j * block : (j + 1) * block]
        if j:
            right = stack([flip(factor[j, k]) for k in range(j)], 0)
            rest = rest - dot_split(stack(new, 1), right)
        result = dot_split(split(rest), inverse[j])
        new.append(split(result))
        half = blocks // 2
        mine = right_side == j // half
        place = pl.ds((j % half) * block, block)

        @pl.when(mine)
        def _():
            keep_ref[:, place] = result

        @pl.when(jnp.logical_not(mine))
        def _():
            give_ref[:, place] = result


def recur(index, partial, mine, other, inv_tiles):
    rows, panel = partial.shape
    blocks = inv_tiles.shape[0]
    rows = rows // SENDS
    half = jax.ShapeDtypeStruct((rows, panel // 2), jnp.float32)
    vmem = pl.BlockSpec(memory_space=pltpu.VMEM)
    return pl.pallas_call(
        functools.partial(recur_kernel, blocks),
        grid=(1,),
        in_specs=[pl.BlockSpec((rows, panel), lambda i: (index, 0)), vmem, vmem, vmem],
        out_specs=[vmem, vmem],
        out_shape=[half, half],
        compiler_params=pltpu.CompilerParams(vmem_limit_bytes=20 << 20),
        name="recur",
    )(*near([partial, mine, other]), inv_tiles)


def finish_kernel(keep_ref, taken_ref, *refs):
    refs[-1][...] = keep_ref[...] + taken_ref[...]


def finish(index, keep, taken, result):
    rows, columns = keep.shape
    vmem = pl.BlockSpec(memory_space=pltpu.VMEM)
    anywhere = pl.BlockSpec(memory_space=pl.ANY)
    old = [] if result is None else [result]
    return pl.pallas_call(
        finish_kernel,
        grid=(1,),
        in_specs=[vmem, vmem] + [anywhere] * len(old),
        out_specs=pl.BlockSpec((rows, columns), lambda i: (index, 0)),
        out_shape=jax.ShapeDtypeStruct((rows * SENDS, columns), jnp.float32),
        input_output_aliases={2: 0} if old else {},
        compiler_params=pltpu.CompilerParams(vmem_limit_bytes=8 << 20),
        name="finish",
    )(*near([keep, taken]), *old)


def lined(*args):
    return lined_panel(*args)


def lined_panel(coeffs, earlier, inv_tiles, piv_local, piv_owner):
    size = lax.axis_size("wide")
    lines = size // GROUP
    me = lax.axis_index("wide")
    panel = piv_local.shape[0]
    block = inv_tiles.shape[1]
    blocks = inv_tiles.shape[0]
    capacity = 3 * panel // size
    widths = [source.shape[1] // size for source in (coeffs, earlier)]
    edge = GROUP * widths[0]

    owners = piv_owner[:, 0]
    positions = jnp.arange(panel, dtype=jnp.int32)
    earlier_same = (owners[:, None] == owners[None, :]) & (positions[None, :] < positions[:, None])
    ranks = jnp.sum(earlier_same, axis=1, dtype=jnp.int32)
    hops = tuple(range(lines - 1, -1, -1))
    cuts = (hops,) if ONE_CUT else (hops[: lines // 2], hops[lines // 2 :])
    parts = {}
    for hops in cuts:
        made = cut(hops, lines, capacity, piv_owner, piv_local, coeffs, earlier)
        for index, hop in enumerate(hops):
            for bit in range(GROUP):
                parts[hop * GROUP + bit] = made[index * GROUP + bit]
    got = []
    for bit in range(size):
        got.append(exchange(parts[bit], "wide", bit, size) if bit else parts[bit])
    stacked = jnp.concatenate(got, axis=0)
    places = (owners ^ me) * capacity + ranks
    taken = places[:, None] == jnp.arange(size * capacity, dtype=jnp.int32)[None, :]
    own = lax.dot_general(
        stacked,
        taken.astype(jnp.bfloat16),
        (((0,), (1,)), ((), ())),
        preferred_element_type=jnp.float32,
    ).astype(jnp.bfloat16)

    def swap_middle(value):
        pairs = [(i, i ^ (3 * GROUP)) for i in range(size) if i // GROUP in (1, 2)]
        return lax.ppermute(value, "wide", pairs)

    def send_out(value):
        pairs = [(i, i ^ GROUP) for i in range(size) if i // GROUP in (1, 2)]
        return lax.ppermute(value, "wide", pairs)

    pair = exchange(own, "wide", GROUP, size)
    middle = swap_middle(own)
    farther = swap_middle(pair)
    out = send_out(middle)
    last_out = send_out(farther)
    table = ["out", "middle", "middle", "out"]
    third = choose(table, {"out": out, "middle": middle})
    fourth = choose(table, {"out": last_out, "middle": farther})
    pieces = [own, pair, third, fourth]
    sources = [(0, 1, 2, 3), (1, 0, 3, 2), (2, 2, 1, 1), (3, 3, 0, 0)]

    groups = []
    for piece in pieces:
        across = exchange(piece, "wide", 2, size)
        beside = exchange(piece, "wide", 1, size)
        corner = exchange(across, "wide", 1, size)
        groups.append([piece, beside, across, corner])
    ticks = {hop: tick(owners if hop % 2 else piv_local, hop) for hop in range(1, lines - 1)}
    pairs = len(lower_pairs(blocks)[0])
    mine = jnp.zeros((pairs, block, block), jnp.float32)
    mine = lower_only(blocks, edge, tuple(range(GROUP)), mine, groups[0])
    steps = (("narrow", 1), ("wide", 2 * GROUP), ("wide", GROUP))
    for axis, bit in steps:
        mine = mine + exchange(mine, axis, bit, lax.axis_size(axis))
    state = None
    for index, (source, group) in enumerate(zip(sources, groups)):
        ticked = ticks[min(max(index, 1), lines - 2)]
        state = accumulate(source, blocks, ticked, coeffs, earlier, group, state, True)
    other = exchange(mine, "wide", 1, size)
    result = None
    for index in range(SENDS):
        keep, give = recur(index, state[0], mine, other, inv_tiles)
        taken = exchange(give, "narrow", 1, 2)
        result = finish(index, keep, taken, result)
    return result


def on_device(coeffs, earlier, inv_tiles, piv_local, piv_owner):
    chosen = lined if fits(coeffs, earlier, inv_tiles) else general
    return chosen(coeffs, earlier, inv_tiles, piv_local, piv_owner)


def fits(coeffs, earlier, inv_tiles):
    size = lax.axis_size("wide")
    lines = size // GROUP
    return (
        size == lines * GROUP
        and size & (size - 1) == 0
        and lines == 4
        and lax.axis_size("narrow") == 2
        and coeffs.shape[0] % (SUBLANES * TILES) == 0
        and coeffs.shape[1] % (lines * LANES) == 0
        and earlier.shape[1] % (lines * LANES) == 0
        and (coeffs.shape[1] + earlier.shape[1]) % (size * SUBLANES) == 0
        and inv_tiles.shape[0] % 4 == 0
    )


def solution(mesh):
    return jax.shard_map(
        on_device,
        mesh=mesh,
        in_specs=(P("wide", "narrow"), P("wide", "narrow"), P(), P(), P()),
        out_specs=P("wide", "narrow"),
        check_vma=False,
    )
```
